32 devices in a mesh: grp: 4 (over y, core), rep: 2 (over x), mp: 4 (over z).
Axes of the slice: x: 2, y: 2, z: 4, core: 2. Of those that a mesh axis runs over, the one named last changes fastest.
Arguments:
- inputs: bfloat16 [16, 8192], P('grp', 'rep'), may hold values from -6 to 6
- stale_rows: int32 [16], P('grp'), may hold values 0 or 1
- row_order: int32 [16], P('grp'), may hold values from 0 to 3, as said below
- lengths: int32 [16], P(('grp', 'rep')), may hold values from 2 to 1024
- old_q: bfloat16 [8192, 64, 128], P('rep', 'mp'), may hold values from -0.0625 to 0.0625
- old_kv: bfloat16 [8192, 16, 128], P('rep', 'mp'), may hold values from -0.0625 to 0.0625
- fresh_q: bfloat16 [8192, 64, 128], P('rep', 'mp', 'grp'), may hold values from -0.0625 to 0.0625
- fresh_kv: bfloat16 [8192, 16, 128], P('rep', 'mp', 'grp'), may hold values from -0.0625 to 0.0625
- key_cache: bfloat16 [16, 1024, 8, 128], P(('grp', 'rep'), 'mp'), may hold values from -320 to 320
- value_cache: bfloat16 [16, 1024, 8, 128], P(('grp', 'rep'), 'mp'), may hold values from -6 to 6
Outputs:
- attention: bfloat16 [16, 64, 128], P(('grp', 'rep'), 'mp')
The draws below stay inside these ranges and needn't reach their ends.
Inputs may be any that keep to these rules, and one draw needn't show every extreme that they name: `row_order`: within each group of 4 consecutive entries, a permutation of 0 to 3; entry i names the cache row of the group's i-th shortest row by lengths, ties by cache row.
All inputs are finite; a program needn't handle non-finite values. No bound on the sum of `stale_rows` on one device may be relied on, other than what follows from the above.
Results may differ from the reference program's by a relative error of at most 0.017.
Values may be sent and summed in bfloat16 or wider, within the bound.
No kernel may reach another device: no remote copies, remote signals or barrier semaphores. Data moves between devices by JAX's collectives and lax.ppermute only.
A program may use at most 128 MiB of HBM per device.

```python
import math
import jax
import jax.numpy as jnp
from jax import lax

D = 8192
H = 64
KVH = 8
HD = 128
KVS = 16
ROWS_GRP = 4
ROWS = 16
CTX = 1024
N_GRP = 4


def rows_and_order(key):
    base = jax.random.fold_in(key, 5)
    row_lengths = jax.random.randint(base, (ROWS,), 2, CTX + 1, dtype=jnp.int32)
    ranked = row_lengths.reshape(N_GRP, ROWS_GRP) * ROWS_GRP + jnp.arange(ROWS_GRP, dtype=jnp.int32)[None, :]
    ordering = jnp.argsort(ranked, axis=1).astype(jnp.int32).reshape(ROWS)
    return (row_lengths, ordering)


def draw_lengths(key, part):
    return rows_and_order(key)[0]


def draw_row_order(key, part):
    return rows_and_order(key)[1]


def draw_key_cache(key, part):
    leading_key_sample = jax.random.fold_in(jax.random.fold_in(key, 9), 0)
    values = jax.random.truncated_normal(leading_key_sample, -6.0, 6.0, (ROWS, CTX, KVH, HD), jnp.float32)
    return values.astype(jnp.bfloat16)


def set_ends(array, rng, low, largest):
    extent = array.shape
    place = [jax.random.randint(jax.random.fold_in(rng, axis), (), 0, extent[axis]) for axis in range(len(extent))]
    array = array.at[tuple(place)].set(low)
    longest = extent.index(max(extent))
    place[longest] = (place[longest] + 1) % extent[longest]
    return array.at[tuple(place)].set(largest)


def shard_levels(own_key, shape, cuts, smallest, largest):
    gain = 1.0
    for dim, shards_of in cuts:
        heights = jax.random.uniform(jax.random.fold_in(jax.random.fold_in(own_key, 6), dim), (shards_of,), jnp.float32, smallest / len(cuts), largest / len(cuts))
        gain = gain * jnp.repeat(jnp.exp(heights), shape[dim] // shards_of).reshape((-1,) + (1,) * (len(shape) - 1 - dim))
    return gain


def scatter_about(own_key, extent, spread, limit, shards=(), held_as=jnp.bfloat16):
    loudness = shard_levels(own_key, extent, shards, -0.22, 0.18) if shards else 1.0
    values = jax.random.normal(own_key, extent, jnp.float32) * spread * loudness
    return jnp.minimum(jnp.maximum(values, -limit), limit).astype(held_as)


def setup_inputs(seed: int = 0) -> dict:
    arg_keys = jax.random.split(jax.random.key(seed), 11)
    return {
        "inputs": scatter_about(arg_keys[0], (ROWS, D), 1.0, 6.0, ((0, 4), (1, 2))),
        "stale_rows": set_ends((jax.random.randint(arg_keys[1], (ROWS,), 0, 2) < 1).astype(jnp.int32), jax.random.fold_in(arg_keys[1], 1), 0, 1),
        "row_order": draw_row_order(jax.random.fold_in(arg_keys[10], 71), 0),
        "lengths": draw_lengths(jax.random.fold_in(arg_keys[10], 71), 0),
        "old_q": scatter_about(arg_keys[4], (D, H, HD), D ** -0.5, 0.0625, ((0, 2), (1, 4))),
        "old_kv": scatter_about(arg_keys[5], (D, KVS, HD), D ** -0.5, 0.0625, ((0, 2), (1, 4))),
        "fresh_q": scatter_about(arg_keys[6], (D, H, HD), D ** -0.5, 0.0625, ((0, 2), (1, 4), (2, 4))),
        "fresh_kv": scatter_about(arg_keys[7], (D, KVS, HD), D ** -0.5, 0.0625, ((0, 2), (1, 4), (2, 4))),
        "key_cache": draw_key_cache(jax.random.fold_in(arg_keys[10], 71), 0),
        "value_cache": scatter_about(arg_keys[9], (ROWS, CTX, KVH, HD), 1.0, 6.0, ((0, 8), (1, 4))),
    }


def attend(pieces):
    queries, incoming_keys, new_values, cached_keys, cached_values, row_lengths = pieces
    row_count = queries.shape[0]
    per_group = H // KVH
    rescale_multiplier = 1.0 / math.sqrt(HD)
    grouped_query_rows = queries.astype(jnp.float32).reshape(row_count, KVH, per_group, HD)
    scores = jnp.einsum('bkgd,blkd->bkgl', grouped_query_rows, cached_keys.astype(jnp.float32)) * rescale_multiplier
    allowed = (jnp.arange(CTX).astype(jnp.int32)[None, :] < row_lengths[:, None])[:, None, None, :]
    incoming_score = jnp.einsum('stfz,stz->stf', grouped_query_rows, incoming_keys.astype(jnp.float32)) * rescale_multiplier
    row_top = jnp.maximum(lax.optimization_barrier(jnp.max(jnp.where(allowed, scores, -1e+30), axis=-1)), incoming_score)
    probable = jnp.where(allowed, jnp.exp(scores - row_top[..., None]), jnp.float32(0.0))
    new_weight = jnp.exp(incoming_score - row_top)
    softmax_divisor = lax.optimization_barrier(jnp.sum(probable, axis=-1)) + new_weight
    rounded = lax.optimization_barrier(probable.astype(jnp.bfloat16)).astype(jnp.float32)
    numerator = jnp.einsum('bkgl,blkd->bkgd', rounded, cached_values.astype(jnp.float32))
    numerator = numerator + new_weight[..., None] * new_values.astype(jnp.float32)[:, :, None, :]
    return (numerator / softmax_divisor[..., None]).astype(jnp.bfloat16).reshape(row_count, H, HD)

def reference(inputs, stale_rows, row_order, lengths, old_q, old_kv, fresh_q, fresh_kv, key_cache, value_cache):
    inverse = jnp.argsort(row_order.reshape(N_GRP, ROWS_GRP), axis=1).astype(jnp.int32)
    slot_inputs = jnp.take_along_axis(inputs.reshape(N_GRP, ROWS_GRP, D), inverse[:, :, None], axis=1)
    slot_inputs = slot_inputs.reshape(ROWS, D).astype(jnp.float32)
    slot_stale = jnp.take_along_axis(stale_rows.reshape(N_GRP, ROWS_GRP), inverse, axis=1).reshape(ROWS, 1)

    def project(old_weight, fresh_weight, column_heads):
        old_part = jnp.dot(slot_inputs, old_weight.reshape(D, column_heads * HD).astype(jnp.float32))
        new_part = jnp.dot(slot_inputs, fresh_weight.reshape(D, column_heads * HD).astype(jnp.float32))
        return jnp.where(slot_stale == 1, old_part, new_part).astype(jnp.bfloat16)
    queries = project(old_q, fresh_q, H).reshape(ROWS, H, HD)
    new_slots = project(old_kv, fresh_kv, KVS).reshape(ROWS, KVS, HD)
    incoming_keys = new_slots[:, :KVH]
    new_values = new_slots[:, KVH:]
    result = lax.map(attend, (queries.reshape(N_GRP, ROWS_GRP, H, HD), incoming_keys.reshape(N_GRP, ROWS_GRP, KVH, HD), new_values.reshape(N_GRP, ROWS_GRP, KVH, HD), key_cache.reshape(N_GRP, ROWS_GRP, CTX, KVH, HD), value_cache.reshape(N_GRP, ROWS_GRP, CTX, KVH, HD), lengths.reshape(N_GRP, ROWS_GRP)))
    return result.reshape(ROWS, H, HD)
```

```python
import functools
import math

import jax
import jax.numpy as jnp
from jax import lax
from jax.sharding import PartitionSpec as P

AXES = ("grp", "rep", "mp")


def slot_order(inputs, stale_rows, row_order):
    lanes = 128
    flags = jnp.broadcast_to(stale_rows.astype(inputs.dtype)[:, None], (inputs.shape[0], lanes))
    rows = jnp.concatenate([inputs, flags], axis=1)
    slots = jnp.arange(inputs.shape[0], dtype=row_order.dtype)
    moved = 0
    for i in range(inputs.shape[0]):
        moved = moved + jnp.where((slots == row_order[i])[:, None], rows[i][None], 0)
    return moved


def plain(
    sizes, inputs, stale_rows, row_order, lengths, old_q, old_kv, fresh_q, fresh_kv, key_cache, value_cache
):
    n_grp, n_rep, n_mp = sizes
    part_width = inputs.shape[1]
    heads_here = old_q.shape[1]
    head_size = old_q.shape[2]
    slice_here = fresh_q.shape[2]
    slots_here = heads_here + old_kv.shape[1]
    gathered = lax.all_gather(slot_order(inputs, stale_rows, row_order), "grp", axis=0, tiled=True)
    rows_all = gathered.shape[0]
    features = gathered[:, :part_width]
    stale = gathered[:, part_width] == 1
    first = lax.axis_index("grp") * slice_here

    def project(q, kv):
        parts = [jnp.einsum("bf,fhd->bhd", features, w, preferred_element_type=jnp.float32) for w in (q, kv)]
        return jnp.concatenate(parts, axis=1)

    cut = functools.partial(lax.dynamic_slice_in_dim, start_index=first, slice_size=slice_here, axis=2)
    terms = jnp.where(stale[:, None, None], project(cut(old_q), cut(old_kv)), project(fresh_q, fresh_kv))
    rows_here = rows_all // (n_grp * n_rep)
    terms = terms.reshape(n_grp * n_rep, 1, rows_here * slots_here * slice_here)
    terms = jnp.broadcast_to(terms, (n_grp * n_rep, n_mp, terms.shape[2]))
    terms = terms.reshape(n_grp * n_rep * n_mp, 1, terms.shape[2])
    held = lax.all_to_all(terms, AXES, 0, 0, tiled=True)
    held = held.reshape(n_grp, n_rep, n_mp, rows_here, slots_here, slice_here)
    held = jnp.sum(held, axis=1).astype(jnp.bfloat16)
    held = jnp.transpose(held, (2, 1, 3, 0, 4)).reshape(rows_here, n_mp, slots_here, head_size)
    queries = held[:, :, :heads_here].reshape(rows_here, n_mp * heads_here, head_size)
    slots = held[:, :, heads_here:].reshape(rows_here, -1, head_size)
    kv_heads = slots.shape[1] // 2
    head_count = queries.shape[1]
    per_group = head_count // kv_heads
    scale = 1.0 / math.sqrt(head_size)
    grouped = queries.reshape(rows_here, kv_heads, per_group, head_size)
    scores = jnp.einsum("bkgd,blkd->bkgl", grouped, key_cache, preferred_element_type=jnp.float32) * scale
    positions_here = key_cache.shape[1]
    positions = lax.axis_index("mp") * positions_here + jnp.arange(positions_here, dtype=jnp.int32)
    allowed = (positions[None, :] < lengths[:, None])[:, None, None, :]
    new_keys = slots[:, :kv_heads, None].astype(jnp.float32)
    new_values = slots[:, kv_heads:, None].astype(jnp.float32)
    new_score = jnp.sum(grouped.astype(jnp.float32) * new_keys, axis=-1) * scale
    new_score = jnp.where(lax.axis_index("mp") == 0, new_score, -1e30)
    top = jnp.maximum(jnp.max(jnp.where(allowed, scores, -1e30), axis=-1), new_score)
    probable = jnp.where(allowed, jnp.exp(scores - top[..., None]), 0.0)
    new_weight = jnp.where(lax.axis_index("mp") == 0, jnp.exp(new_score - top), 0.0)
    total = jnp.sum(probable, axis=-1) + new_weight
    out = jnp.einsum("bkgl,blkd->bkgd", probable.astype(jnp.bfloat16), value_cache, preferred_element_type=jnp.float32)
    out = out + new_weight[..., None] * new_values
    flat = (rows_here, head_count)
    part = jnp.concatenate(
        [out.reshape(*flat, head_size), top.reshape(*flat, 1), total.reshape(*flat, 1)], axis=2
    )
    part = lax.all_to_all(part[None], "mp", split_axis=2, concat_axis=0, tiled=True)
    outs, tops, totals = part[..., :head_size], part[..., head_size], part[..., head_size + 1]
    weights = jnp.exp(tops - jnp.max(tops, axis=0)[None])
    numerator = jnp.sum(outs * weights[..., None], axis=0)
    return (numerator / jnp.sum(totals * weights, axis=0)[..., None]).astype(jnp.bfloat16)


def solution(mesh):
    sizes = tuple(mesh.shape[a] for a in AXES)
    return jax.shard_map(
        functools.partial(plain, sizes),
        mesh=mesh,
        in_specs=(
            P("grp", "rep"),
            P("grp"),
            P("grp"),
            P(("grp", "rep")),
            P("rep", "mp", None),
            P("rep", "mp", None),
            P("rep", "mp", "grp"),
            P("rep", "mp", "grp"),
            P(("grp", "rep"), "mp", None, None),
            P(("grp", "rep"), "mp", None, None),
        ),
        out_specs=P(("grp", "rep"), "mp", None),
        check_vma=False,
    )
```

```python
import functools
import math

import jax
import jax.numpy as jnp
from jax import lax
from jax.experimental import pallas as pl
from jax.experimental.pallas import tpu as pltpu
from jax.sharding import PartitionSpec as P

AXES = ("grp", "rep", "mp")


def slot_order(inputs, stale_rows, row_order):
    lanes = 128
    flags = jnp.broadcast_to(stale_rows.astype(inputs.dtype)[:, None], (inputs.shape[0], lanes))
    rows = jnp.concatenate([inputs, flags], axis=1)
    slots = jnp.arange(inputs.shape[0], dtype=row_order.dtype)
    moved = 0
    for i in range(inputs.shape[0]):
        moved = moved + jnp.where((slots == row_order[i])[:, None], rows[i][None], 0)
    return moved


def plain(
    sizes, inputs, stale_rows, row_order, lengths, old_q, old_kv, fresh_q, fresh_kv, key_cache, value_cache
):
    n_grp, n_rep, n_mp = sizes
    part_width = inputs.shape[1]
    heads_here = old_q.shape[1]
    head_size = old_q.shape[2]
    slice_here = fresh_q.shape[2]
    slots_here = heads_here + old_kv.shape[1]
    gathered = lax.all_gather(slot_order(inputs, stale_rows, row_order), "grp", axis=0, tiled=True)
    rows_all = gathered.shape[0]
    features = gathered[:, :part_width]
    stale = gathered[:, part_width] == 1
    first = lax.axis_index("grp") * slice_here

    def project(q, kv):
        parts = [jnp.einsum("bf,fhd->bhd", features, w, preferred_element_type=jnp.float32) for w in (q, kv)]
        return jnp.concatenate(parts, axis=1)

    cut = functools.partial(lax.dynamic_slice_in_dim, start_index=first, slice_size=slice_here, axis=2)
    terms = jnp.where(stale[:, None, None], project(cut(old_q), cut(old_kv)), project(fresh_q, fresh_kv))
    rows_here = rows_all // (n_grp * n_rep)
    terms = terms.reshape(n_grp * n_rep, 1, rows_here * slots_here * slice_here)
    terms = jnp.broadcast_to(terms, (n_grp * n_rep, n_mp, terms.shape[2]))
    terms = terms.reshape(n_grp * n_rep * n_mp, 1, terms.shape[2])
    held = lax.all_to_all(terms, AXES, 0, 0, tiled=True)
    held = held.reshape(n_grp, n_rep, n_mp, rows_here, slots_here, slice_here)
    held = jnp.sum(held, axis=1).astype(jnp.bfloat16)
    held = jnp.transpose(held, (2, 1, 3, 0, 4)).reshape(rows_here, n_mp, slots_here, head_size)
    queries = held[:, :, :heads_here].reshape(rows_here, n_mp * heads_here, head_size)
    slots = held[:, :, heads_here:].reshape(rows_here, -1, head_size)
    kv_heads = slots.shape[1] // 2
    head_count = queries.shape[1]
    per_group = head_count // kv_heads
    scale = 1.0 / math.sqrt(head_size)
    grouped = queries.reshape(rows_here, kv_heads, per_group, head_size)
    scores = jnp.einsum("bkgd,blkd->bkgl", grouped, key_cache, preferred_element_type=jnp.float32) * scale
    positions_here = key_cache.shape[1]
    positions = lax.axis_index("mp") * positions_here + jnp.arange(positions_here, dtype=jnp.int32)
    allowed = (positions[None, :] < lengths[:, None])[:, None, None, :]
    new_keys = slots[:, :kv_heads, None].astype(jnp.float32)
    new_values = slots[:, kv_heads:, None].astype(jnp.float32)
    new_score = jnp.sum(grouped.astype(jnp.float32) * new_keys, axis=-1) * scale
    new_score = jnp.where(lax.axis_index("mp") == 0, new_score, -1e30)
    top = jnp.maximum(jnp.max(jnp.where(allowed, scores, -1e30), axis=-1), new_score)
    probable = jnp.where(allowed, jnp.exp(scores - top[..., None]), 0.0)
    new_weight = jnp.where(lax.axis_index("mp") == 0, jnp.exp(new_score - top), 0.0)
    total = jnp.sum(probable, axis=-1) + new_weight
    out = jnp.einsum("bkgl,blkd->bkgd", probable.astype(jnp.bfloat16), value_cache, preferred_element_type=jnp.float32)
    out = out + new_weight[..., None] * new_values
    flat = (rows_here, head_count)
    part = jnp.concatenate(
        [out.reshape(*flat, head_size), top.reshape(*flat, 1), total.reshape(*flat, 1)], axis=2
    )
    part = lax.all_to_all(part[None], "mp", split_axis=2, concat_axis=0, tiled=True)
    outs, tops, totals = part[..., :head_size], part[..., head_size], part[..., head_size + 1]
    weights = jnp.exp(tops - jnp.max(tops, axis=0)[None])
    numerator = jnp.sum(outs * weights[..., None], axis=0)
    return (numerator / jnp.sum(totals * weights, axis=0)[..., None]).astype(jnp.bfloat16)


LANES = 128
SUBLANES = 8
HBM = pltpu.MemorySpace.HBM
VMEM = pltpu.MemorySpace.VMEM
SMEM = pltpu.MemorySpace.SMEM
ROOMY = 67_043_328
START_BYTES = 32 << 20


def whole_block(space):
    return pl.BlockSpec(memory_space=space)


def order_kernel(order_in, stale_in, rows_in, moved, order, stale, rows, sems):
    pairs = ((order_in, order), (stale_in, stale), (rows_in, rows))
    copies = [pltpu.make_async_copy(a, b, sems.at[n]) for n, (a, b) in enumerate(pairs)]
    for copy in copies:
        copy.start()
    for copy in copies:
        copy.wait()
    count, width = rows.shape
    where_row = lax.broadcasted_iota(jnp.int32, (count, 1), 0)
    total = jnp.zeros((count, width), jnp.float32)
    flags = jnp.zeros((count, LANES), jnp.float32)
    for i in range(count):
        here = where_row == order[i]
        total = jnp.where(here, rows[i : i + 1, :].astype(jnp.float32), total)
        flags = jnp.where(here, stale[i].astype(jnp.float32), flags)
    moved[:, :width] = total.astype(moved.dtype)
    moved[:, width:] = flags.astype(moved.dtype)


def load_kernel(old_q, near, sem):
    copy = pltpu.make_async_copy(old_q.at[:, lax.axis_index("grp")], near, sem)
    copy.start()
    copy.wait()


def project_kernel(n_rep, n_mp, *refs):
    rows_in = refs[:-7]
    old_q, old_kv, fresh_q, fresh_kv, out, features, staged = refs[-7:]
    n_grp = len(rows_in)
    mine = lax.axis_index("grp")
    group_rows, width = rows_in[0].shape
    rows = group_rows * n_grp
    part_width = width - LANES
    per_row = old_q.shape[0] // part_width
    for k, part in enumerate(rows_in):
        features[k * group_rows : (k + 1) * group_rows, :] = part[...]
    chunks = part_width // LANES
    stacked = jnp.concatenate([features[:, c * LANES : (c + 1) * LANES] for c in range(chunks)], axis=0)
    spread_width = LANES * per_row
    source = lax.broadcasted_iota(jnp.int32, (LANES, spread_width), 0)
    target = lax.broadcasted_iota(jnp.int32, (LANES, spread_width), 1)
    spread = jnp.where(target // per_row == source, 1.0, 0.0).astype(jnp.bfloat16)
    wide = jnp.dot(stacked, spread, preferred_element_type=jnp.float32).astype(jnp.bfloat16)
    lane = lax.broadcasted_iota(jnp.int32, (1, spread_width), 1) % per_row
    picks = [jnp.where(lane == h, 1.0, 0.0).astype(jnp.bfloat16) for h in range(per_row)]
    old = jnp.zeros((per_row * rows, 2 * LANES), jnp.float32)
    for c in range(chunks):
        piece = wide[c * rows : (c + 1) * rows]
        left = jnp.concatenate([piece * pick for pick in picks], axis=0)
        span = slice(c * spread_width, (c + 1) * spread_width)
        right = jnp.concatenate([old_q[span, :], old_kv[span, :]], axis=1)
        old = old + jnp.dot(left, right, preferred_element_type=jnp.float32)
    values = features[:, :part_width]
    across = (((1,), (1,)), ((), ()))
    new_q = lax.dot_general(values, fresh_q[...], across, preferred_element_type=jnp.float32)
    new_kv = lax.dot_general(values, fresh_kv[...], across, preferred_element_type=jnp.float32)
    stale = features[:, part_width : part_width + 1].astype(jnp.float32) == 1.0
    for j in range(per_row):
        span = slice(j * LANES, (j + 1) * LANES)
        staged[j * rows : (j + 1) * rows, :] = jnp.where(stale, old[j * rows : (j + 1) * rows, :LANES], new_q[:, span])
    kept = old[:rows, LANES:]
    for h in range(1, per_row):
        kept = jnp.where(mine == h, old[h * rows : (h + 1) * rows, LANES:], kept)
    staged[per_row * rows :, :] = jnp.where(stale, kept, new_kv)
    parts = per_row + 1
    rows_here = group_rows // n_rep
    for k in range(n_grp):
        group = jnp.bitwise_xor(mine, k)
        for r in range(n_rep):
            for i in range(rows_here):
                row = k * group_rows + r * rows_here + i
                block = staged[pl.ds(row, parts, stride=rows), :]
                for m in range(n_mp):
                    first = (m * rows_here + i) * parts
                    out[group * n_rep + r, first : first + parts, :] = block


def attend_kernel(sizes, scale, order, stale, lengths, held, keys, values, *refs):
    n_grp, n_rep, n_mp = sizes
    outs = refs[:n_mp]
    summed, turned, queries, slots, packed = refs[n_mp:]
    rows_here, places, head_size = keys.shape
    slots_here = n_grp
    heads_here = queries.shape[0] // (rows_here * n_mp)
    head_count = heads_here * n_mp
    kv_heads = slots_here * n_mp // 2
    per_group = head_count // kv_heads
    shares = heads_here // n_grp
    parts = shares + 1
    block = held.shape[1]
    step = head_size // n_grp
    mp = lax.axis_index("mp")
    rep = lax.axis_index("rep")
    sums = []
    for g in range(n_grp):
        total = held[g * n_rep]
        for r in range(1, n_rep):
            total = total + held[g * n_rep + r]
        sums.append(total)
        summed[g * block : (g + 1) * block, :] = total
    lane = lax.broadcasted_iota(jnp.int32, (1, head_size), 1) // step
    for h in range(n_grp):
        total = sums[h]
        for g in range(n_grp):
            if g != h:
                total = jnp.where(lane == g, pltpu.roll(sums[g], (step * (g - h)) % head_size, 1), total)
        turned[h * block : (h + 1) * block, :] = total
    lanes = lax.broadcasted_iota(jnp.int32, (SUBLANES, places), 1)
    stats_lane = lax.broadcasted_iota(jnp.int32, (1, LANES), 1) // (LANES // (2 * rows_here))
    stats = [jnp.zeros((per_group, LANES), jnp.float32) for _ in range(kv_heads)]
    for i in range(rows_here):
        flag = jnp.int32(0)
        for n in range(order.shape[0]):
            flag = jnp.where(order[n] == rep * rows_here + i, stale[n], flag)

        @pl.when(flag == 1)
        def _():
            for m in range(n_mp):
                base = (m * rows_here + i) * parts
                for g in range(n_grp):
                    first = i * head_count + m * heads_here + g * shares
                    queries[first : first + shares, :] = summed[g * block + base : g * block + base + shares, :]
                first = i * n_mp * slots_here + m * slots_here
                slots[first : first + slots_here, :] = summed[pl.ds(base + shares, slots_here, stride=block), :]

        @pl.when(flag != 1)
        def _():
            for m in range(n_mp):
                base = (m * rows_here + i) * parts
                for j in range(shares):
                    first = i * head_count + m * heads_here + j * n_grp
                    queries[first : first + n_grp, :] = turned[pl.ds(base + j, n_grp, stride=block), :]
                first = i * n_mp * slots_here + m * slots_here
                slots[first : first + slots_here, :] = turned[pl.ds(base + shares, slots_here, stride=block), :]

        query = queries[i * head_count : (i + 1) * head_count, :].astype(jnp.bfloat16)
        fresh = slots[i * 2 * kv_heads : (i + 1) * 2 * kv_heads, :].astype(jnp.bfloat16).astype(jnp.float32)
        scores = lax.dot_general(query, keys[i], (((1,), (1,)), ((), ())), preferred_element_type=jnp.float32) * scale
        position = mp * (places // kv_heads) + lanes // kv_heads
        valid = position < lengths[i]
        weights, tops, totals, added = [], [], [], []
        for b in range(kv_heads):
            span = slice(b * per_group, (b + 1) * per_group)
            allowed = valid & (lanes % kv_heads == b)
            mine = jnp.sum(query[span].astype(jnp.float32) * fresh[b : b + 1], axis=1, keepdims=True) * scale
            mine = jnp.where(mp == 0, mine, -1e30)
            top = jnp.max(jnp.where(allowed, scores[span], -1e30), axis=1, keepdims=True)
            top = jnp.maximum(top, mine)
            probable = jnp.where(allowed, jnp.exp(scores[span] - top), 0.0)
            own = jnp.where(mp == 0, jnp.exp(mine - top), 0.0)
            total = jnp.sum(probable, axis=1, keepdims=True) + own
            weights.append(probable)
            added.append(own * fresh[kv_heads + b : kv_heads + b + 1])
            stats[b] = jnp.where(stats_lane == 2 * i, top, stats[b])
            stats[b] = jnp.where(stats_lane == 2 * i + 1, total, stats[b])
        weight = jnp.concatenate(weights, axis=0).astype(jnp.bfloat16)
        out = jnp.dot(weight, values[i], preferred_element_type=jnp.float32) + jnp.concatenate(added, axis=0)
        for m in range(n_mp):
            packed[m, i * heads_here : (i + 1) * heads_here, :] = out[m * heads_here : (m + 1) * heads_here]
    for m in range(n_mp):
        here = jnp.concatenate(stats[m * heads_here // per_group : (m + 1) * heads_here // per_group], axis=0)
        packed[m, rows_here * heads_here :, :] = here
    for k, ref in enumerate(outs):
        ref[...] = packed[jnp.bitwise_xor(mp, k)]


def join_kernel(*refs):
    parts, out = refs[:-1], refs[-1]
    rows_here, heads_here, head_size = out.shape
    step = LANES // (2 * rows_here)
    stats = rows_here * heads_here
    for i in range(rows_here):
        tops = [p[stats:, 2 * i * step : 2 * i * step + 1] for p in parts]
        sums = [p[stats:, (2 * i + 1) * step : (2 * i + 1) * step + 1] for p in parts]
        joined = functools.reduce(jnp.maximum, tops)
        scales = [jnp.exp(top - joined) for top in tops]
        numerator = sum(p[i * heads_here : (i + 1) * heads_here, :] * s for p, s in zip(parts, scales))
        divisor = sum(n * s for n, s in zip(sums, scales))
        out[i] = (numerator / divisor).astype(out.dtype)


def exchanged(value, axis, count):
    return [value] + [lax.ppermute(value, axis, [(i, i ^ k) for i in range(count)]) for k in range(1, count)]


def close(
    sizes, inputs, stale_rows, row_order, lengths, old_q, old_kv, fresh_q, fresh_kv, key_cache, value_cache
):
    n_grp, n_rep, n_mp = sizes
    group_rows, part_width = inputs.shape
    heads_here = old_q.shape[1]
    head_size = old_q.shape[2]
    slice_here = fresh_q.shape[2]
    rows = group_rows * n_grp
    rows_here, positions_here, kv_heads, _ = key_cache.shape
    shares = heads_here // n_grp
    parts = shares + 1
    bf16 = functools.partial(jax.ShapeDtypeStruct, dtype=jnp.bfloat16)
    f32 = functools.partial(jax.ShapeDtypeStruct, dtype=jnp.float32)
    moved = pl.pallas_call(
        order_kernel,
        out_shape=bf16((group_rows, part_width + LANES)),
        in_specs=[whole_block(HBM)] * 3,
        out_specs=whole_block(VMEM),
        scratch_shapes=[
            pltpu.SMEM((group_rows,), jnp.int32),
            pltpu.SMEM((group_rows,), jnp.int32),
            pltpu.VMEM((group_rows, part_width), jnp.bfloat16),
            pltpu.SemaphoreType.DMA((3,)),
        ],
        compiler_params=pltpu.CompilerParams(vmem_limit_bytes=ROOMY),
        cost_estimate=pl.CostEstimate(flops=0, bytes_accessed=START_BYTES, transcendentals=0),
        name="order",
    )(row_order, stale_rows, inputs)
    gathered = exchanged(moved, "grp", n_grp)
    share = bf16((part_width, shares, head_size))
    near_q = pl.pallas_call(
        load_kernel,
        out_shape=share,
        in_specs=[whole_block(HBM)],
        out_specs=whole_block(pl.ANY),
        scratch_shapes=[pltpu.SemaphoreType.DMA],
        compiler_params=pltpu.CompilerParams(vmem_limit_bytes=40 << 20),
        cost_estimate=pl.CostEstimate(flops=0, bytes_accessed=4 * math.prod(share.shape), transcendentals=0),
        name="load",
    )(old_q.reshape(part_width, n_grp, shares, head_size))
    near = (
        old_kv.reshape(part_width * n_grp, head_size),
        jnp.transpose(fresh_q, (1, 2, 0)).reshape(heads_here * slice_here, part_width),
        jnp.transpose(fresh_kv, (1, 2, 0)).reshape(n_grp * slice_here, part_width),
    )
    block = n_mp * rows_here * parts
    terms = pl.pallas_call(
        functools.partial(project_kernel, n_rep, n_mp),
        out_shape=f32((n_grp * n_rep, block, head_size)),
        in_specs=[whole_block(VMEM)] * (n_grp + 4),
        out_specs=whole_block(VMEM),
        scratch_shapes=[
            pltpu.VMEM((rows, part_width + LANES), jnp.bfloat16),
            pltpu.VMEM((rows * parts, LANES), jnp.float32),
        ],
        compiler_params=pltpu.CompilerParams(vmem_limit_bytes=24 << 20),
        name="project",
    )(*gathered, near_q.reshape(part_width * shares, head_size), *near)
    devices = n_grp * n_rep * n_mp
    held = lax.all_to_all(terms.reshape(devices, 1, rows_here * parts * head_size), AXES, 0, 0, tiled=True)
    held = held.reshape(n_grp * n_rep, block, head_size)
    places = positions_here * kv_heads
    packed_rows = (rows_here + 1) * heads_here
    partial_out = pl.pallas_call(
        functools.partial(attend_kernel, sizes, 1.0 / math.sqrt(head_size)),
        out_shape=[f32((packed_rows, LANES))] * n_mp,
        in_specs=[whole_block(SMEM)] * 3 + [whole_block(VMEM)] * 3,
        out_specs=[whole_block(VMEM)] * n_mp,
        scratch_shapes=[
            pltpu.VMEM((n_grp * block, LANES), jnp.float32),
            pltpu.VMEM((n_grp * block, LANES), jnp.float32),
            pltpu.VMEM((rows_here * heads_here * n_mp, LANES), jnp.float32),
            pltpu.VMEM((rows_here * 2 * kv_heads, LANES), jnp.float32),
            pltpu.VMEM((n_mp, packed_rows, LANES), jnp.float32),
        ],
        compiler_params=pltpu.CompilerParams(vmem_limit_bytes=16 << 20),
        name="attend",
    )(
        row_order,
        stale_rows,
        lengths,
        held,
        key_cache.reshape(rows_here, places, head_size),
        value_cache.reshape(rows_here, places, head_size),
    )
    pieces = [partial_out[0]] + [
        lax.ppermute(partial_out[k], "mp", [(i, i ^ k) for i in range(n_mp)]) for k in range(1, n_mp)
    ]
    return pl.pallas_call(
        join_kernel,
        out_shape=bf16((rows_here, heads_here, head_size)),
        in_specs=[whole_block(VMEM)] * n_mp,
        out_specs=whole_block(VMEM),
        compiler_params=pltpu.CompilerParams(vmem_limit_bytes=4 << 20),
        name="join",
    )(*pieces)


def fits(sizes, old_q, old_kv, fresh_q, key_cache):
    n_grp, n_rep, n_mp = sizes
    heads_here, head_size = old_q.shape[1:]
    slots_here = old_kv.shape[1]
    rows_here, _, kv_heads, _ = key_cache.shape
    return (
        head_size == LANES
        and slots_here == n_grp
        and heads_here == n_grp * n_grp
        and fresh_q.shape[2] * n_grp == head_size
        and n_grp & (n_grp - 1) == 0
        and n_mp & (n_mp - 1) == 0
        and heads_here * n_mp == SUBLANES * kv_heads
        and heads_here % SUBLANES == 0
        and slots_here * n_mp == 2 * kv_heads
        and n_mp * rows_here * (n_grp + 1) % SUBLANES == 0
        and LANES % (2 * rows_here) == 0
        and n_grp * n_rep * rows_here % (2 * SUBLANES) == 0
    )


def local(sizes, *args):
    old_q, old_kv, fresh_q, key_cache = args[4], args[5], args[6], args[8]
    return (close if fits(sizes, old_q, old_kv, fresh_q, key_cache) else plain)(sizes, *args)


def solution(mesh):
    sizes = tuple(mesh.shape[a] for a in AXES)
    return jax.shard_map(
        functools.partial(local, sizes),
        mesh=mesh,
        in_specs=(
            P("grp", "rep"),
            P("grp"),
            P("grp"),
            P(("grp", "rep")),
            P("rep", "mp", None),
            P("rep", "mp", None),
            P("rep", "mp", "grp"),
            P("rep", "mp", "grp"),
            P(("grp", "rep"), "mp", None, None),
            P(("grp", "rep"), "mp", None, None),
        ),
        out_specs=P(("grp", "rep"), "mp", None),
        check_vma=False,
    )
```

```python
import functools
import math

import jax
import jax.numpy as jnp
from jax import lax
from jax.experimental import pallas as pl
from jax.experimental.pallas import tpu as pltpu
from jax.sharding import PartitionSpec as P

AXES = ("grp", "rep", "mp")


def slot_order(inputs, stale_rows, row_order):
    lanes = 128
    flags = jnp.broadcast_to(stale_rows.astype(inputs.dtype)[:, None], (inputs.shape[0], lanes))
    rows = jnp.concatenate([inputs, flags], axis=1)
    slots = jnp.arange(inputs.shape[0], dtype=row_order.dtype)
    moved = 0
    for i in range(inputs.shape[0]):
        moved = moved + jnp.where((slots == row_order[i])[:, None], rows[i][None], 0)
    return moved


def plain(
    sizes, inputs, stale_rows, row_order, lengths, old_q, old_kv, fresh_q, fresh_kv, key_cache, value_cache
):
    n_grp, n_rep, n_mp = sizes
    part_width = inputs.shape[1]
    heads_here = old_q.shape[1]
    head_size = old_q.shape[2]
    slice_here = fresh_q.shape[2]
    slots_here = heads_here + old_kv.shape[1]
    gathered = lax.all_gather(slot_order(inputs, stale_rows, row_order), "grp", axis=0, tiled=True)
    rows_all = gathered.shape[0]
    features = gathered[:, :part_width]
    stale = gathered[:, part_width] == 1
    first = lax.axis_index("grp") * slice_here

    def project(q, kv):
        parts = [jnp.einsum("bf,fhd->bhd", features, w, preferred_element_type=jnp.float32) for w in (q, kv)]
        return jnp.concatenate(parts, axis=1)

    cut = functools.partial(lax.dynamic_slice_in_dim, start_index=first, slice_size=slice_here, axis=2)
    terms = jnp.where(stale[:, None, None], project(cut(old_q), cut(old_kv)), project(fresh_q, fresh_kv))
    rows_here = rows_all // (n_grp * n_rep)
    terms = terms.reshape(n_grp * n_rep, 1, rows_here * slots_here * slice_here)
    terms = jnp.broadcast_to(terms, (n_grp * n_rep, n_mp, terms.shape[2]))
    terms = terms.reshape(n_grp * n_rep * n_mp, 1, terms.shape[2])
    held = lax.all_to_all(terms, AXES, 0, 0, tiled=True)
    held = held.reshape(n_grp, n_rep, n_mp, rows_here, slots_here, slice_here)
    held = jnp.sum(held, axis=1).astype(jnp.bfloat16)
    held = jnp.transpose(held, (2, 1, 3, 0, 4)).reshape(rows_here, n_mp, slots_here, head_size)
    queries = held[:, :, :heads_here].reshape(rows_here, n_mp * heads_here, head_size)
    slots = held[:, :, heads_here:].reshape(rows_here, -1, head_size)
    kv_heads = slots.shape[1] // 2
    head_count = queries.shape[1]
    per_group = head_count // kv_heads
    scale = 1.0 / math.sqrt(head_size)
    grouped = queries.reshape(rows_here, kv_heads, per_group, head_size)
    scores = jnp.einsum("bkgd,blkd->bkgl", grouped, key_cache, preferred_element_type=jnp.float32) * scale
    positions_here = key_cache.shape[1]
    positions = lax.axis_index("mp") * positions_here + jnp.arange(positions_here, dtype=jnp.int32)
    allowed = (positions[None, :] < lengths[:, None])[:, None, None, :]
    new_keys = slots[:, :kv_heads, None].astype(jnp.float32)
    new_values = slots[:, kv_heads:, None].astype(jnp.float32)
    new_score = jnp.sum(grouped.astype(jnp.float32) * new_keys, axis=-1) * scale
    new_score = jnp.where(lax.axis_index("mp") == 0, new_score, -1e30)
    top = jnp.maximum(jnp.max(jnp.where(allowed, scores, -1e30), axis=-1), new_score)
    probable = jnp.where(allowed, jnp.exp(scores - top[..., None]), 0.0)
    new_weight = jnp.where(lax.axis_index("mp") == 0, jnp.exp(new_score - top), 0.0)
    total = jnp.sum(probable, axis=-1) + new_weight
    out = jnp.einsum("bkgl,blkd->bkgd", probable.astype(jnp.bfloat16), value_cache, preferred_element_type=jnp.float32)
    out = out + new_weight[..., None] * new_values
    flat = (rows_here, head_count)
    part = jnp.concatenate(
        [out.reshape(*flat, head_size), top.reshape(*flat, 1), total.reshape(*flat, 1)], axis=2
    )
    part = lax.all_to_all(part[None], "mp", split_axis=2, concat_axis=0, tiled=True)
    outs, tops, totals = part[..., :head_size], part[..., head_size], part[..., head_size + 1]
    weights = jnp.exp(tops - jnp.max(tops, axis=0)[None])
    numerator = jnp.sum(outs * weights[..., None], axis=0)
    return (numerator / jnp.sum(totals * weights, axis=0)[..., None]).astype(jnp.bfloat16)


LANES = 128
SUBLANES = 8
HBM = pltpu.MemorySpace.HBM
VMEM = pltpu.MemorySpace.VMEM
SMEM = pltpu.MemorySpace.SMEM
ROOMY = 57000000
LOAD_LIMIT = 40_000_000
PROJECT_LIMIT = 24_000_000
START_BYTES = 32 << 20
SPANS = 4


def whole_block(space):
    return pl.BlockSpec(memory_space=space)


def order_kernel(order_in, stale_in, rows_in, _, moved, order, stale, rows, sems):
    pairs = ((order_in, order), (stale_in, stale), (rows_in, rows))
    copies = [pltpu.make_async_copy(a, b, sems.at[n]) for n, (a, b) in enumerate(pairs)]
    for copy in copies:
        copy.start()
    for copy in copies:
        copy.wait()
    count, width = rows.shape
    where_row = lax.broadcasted_iota(jnp.int32, (count, 1), 0)
    total = jnp.zeros((count, width), jnp.float32)
    flags = jnp.zeros((count, LANES), jnp.float32)
    for i in range(count):
        here = where_row == order[i]
        total = jnp.where(here, rows[i : i + 1, :].astype(jnp.float32), total)
        flags = jnp.where(here, stale[i].astype(jnp.float32), flags)
    moved[:, :width] = total.astype(moved.dtype)
    moved[:, width:] = flags.astype(moved.dtype)


def load_kernel(old_q, *refs):
    near, sem = refs[-2:]
    copy = pltpu.make_async_copy(old_q.at[:, lax.axis_index("grp")], near, sem)
    copy.start()
    copy.wait()


def project_kernel(n_rep, n_mp, *refs):
    rows_in = refs[:-7]
    old_q, old_kv, fresh_q, fresh_kv, out, features, staged = refs[-7:]
    n_grp = len(rows_in)
    mine = lax.axis_index("grp")
    group_rows, width = rows_in[0].shape
    rows = group_rows * n_grp
    part_width = width - LANES
    per_row = old_q.shape[0] // part_width
    for k, part in enumerate(rows_in):
        features[k * group_rows : (k + 1) * group_rows, :] = part[...]
    chunks = part_width // LANES
    stacked = jnp.concatenate([features[:, c * LANES : (c + 1) * LANES] for c in range(chunks)], axis=0)
    spread_width = LANES * per_row
    source = lax.broadcasted_iota(jnp.int32, (LANES, spread_width), 0)
    target = lax.broadcasted_iota(jnp.int32, (LANES, spread_width), 1)
    spread = jnp.where(target // per_row == source, 1.0, 0.0).astype(jnp.bfloat16)
    wide = jnp.dot(stacked, spread, preferred_element_type=jnp.float32).astype(jnp.bfloat16)
    lane = lax.broadcasted_iota(jnp.int32, (1, spread_width), 1) % per_row
    picks = [jnp.where(lane == h, 1.0, 0.0).astype(jnp.bfloat16) for h in range(per_row)]

    def add(weights):
        half = chunks // 2
        sums = []
        for side in range(2):
            total = 0
            for c in range(side * half, (side + 1) * half, SPANS):
                left = []
                for u in range(c, c + SPANS):
                    piece = wide[u * rows : (u + 1) * rows]
                    left.append(jnp.concatenate([piece * pick for pick in picks], axis=0))
                left = jnp.concatenate(left, axis=1)
                right = weights[c * spread_width : (c + SPANS) * spread_width, :]
                total = total + jnp.dot(left, right, preferred_element_type=jnp.float32)
            sums.append(total)
        return sums[0] + sums[1]

    across = (((1,), (1,)), ((), ()))
    kept_kv = add(old_kv)
    values = features[:, :part_width]
    new_q = lax.dot_general(fresh_q[...], values, across, preferred_element_type=jnp.float32).T
    new_kv = lax.dot_general(fresh_kv[...], values, across, preferred_element_type=jnp.float32).T
    kept_q = add(old_q)
    stale = features[:, part_width : part_width + 1].astype(jnp.float32) == 1.0
    for j in range(per_row):
        span = slice(j * LANES, (j + 1) * LANES)
        staged[j * rows : (j + 1) * rows, :] = jnp.where(stale, kept_q[j * rows : (j + 1) * rows], new_q[:, span])
    kept = kept_kv[:rows]
    for h in range(1, per_row):
        kept = jnp.where(mine == h, kept_kv[h * rows : (h + 1) * rows], kept)
    staged[per_row * rows :, :] = jnp.where(stale, kept, new_kv)
    parts = per_row + 1
    rows_here = group_rows // n_rep
    for k in range(n_grp):
        group = jnp.bitwise_xor(mine, k)
        for r in range(n_rep):
            for i in range(rows_here):
                row = k * group_rows + r * rows_here + i
                block = staged[pl.ds(row, parts, stride=rows), :]
                for m in range(n_mp):
                    first = (m * rows_here + i) * parts
                    out[group * n_rep + r, first : first + parts, :] = block


def attend_kernel(sizes, scale, order, stale, lengths, held, keys, values, *refs):
    n_grp, n_rep, n_mp = sizes
    outs = refs[:n_mp]
    summed, turned, queries, slots, packed = refs[n_mp:]
    rows_here, places, head_size = keys.shape
    slots_here = n_grp
    heads_here = queries.shape[0] // (rows_here * n_mp)
    head_count = heads_here * n_mp
    kv_heads = slots_here * n_mp // 2
    per_group = head_count // kv_heads
    shares = heads_here // n_grp
    parts = shares + 1
    block = held.shape[1]
    step = head_size // n_grp
    mp = lax.axis_index("mp")
    rep = lax.axis_index("rep")
    sums = []
    for g in range(n_grp):
        total = held[g * n_rep]
        for r in range(1, n_rep):
            total = total + held[g * n_rep + r]
        sums.append(total)
        summed[g * block : (g + 1) * block, :] = total
    lane = lax.broadcasted_iota(jnp.int32, (1, head_size), 1) // step
    for h in range(n_grp):
        total = sums[h]
        for g in range(n_grp):
            if g != h:
                total = jnp.where(lane == g, pltpu.roll(sums[g], (step * (g - h)) % head_size, 1), total)
        turned[h * block : (h + 1) * block, :] = total
    lanes = lax.broadcasted_iota(jnp.int32, (SUBLANES, places), 1)
    stats_lane = lax.broadcasted_iota(jnp.int32, (1, LANES), 1) // (LANES // (2 * rows_here))
    stats = [jnp.zeros((per_group, LANES), jnp.float32) for _ in range(kv_heads)]
    for i in range(rows_here):
        flag = jnp.int32(0)
        for n in range(order.shape[0]):
            flag = jnp.where(order[n] == rep * rows_here + i, stale[n], flag)

        @pl.when(flag == 1)
        def _():
            for m in range(n_mp):
                base = (m * rows_here + i) * parts
                for g in range(n_grp):
                    first = i * head_count + m * heads_here + g * shares
                    queries[first : first + shares, :] = summed[g * block + base : g * block + base + shares, :]
                first = i * n_mp * slots_here + m * slots_here
                slots[first : first + slots_here, :] = summed[pl.ds(base + shares, slots_here, stride=block), :]

        @pl.when(flag != 1)
        def _():
            for m in range(n_mp):
                base = (m * rows_here + i) * parts
                for j in range(shares):
                    first = i * head_count + m * heads_here + j * n_grp
                    queries[first : first + n_grp, :] = turned[pl.ds(base + j, n_grp, stride=block), :]
                first = i * n_mp * slots_here + m * slots_here
                slots[first : first + slots_here, :] = turned[pl.ds(base + shares, slots_here, stride=block), :]

        query = queries[i * head_count : (i + 1) * head_count, :].astype(jnp.bfloat16)
        fresh = slots[i * 2 * kv_heads : (i + 1) * 2 * kv_heads, :].astype(jnp.bfloat16).astype(jnp.float32)
        scores = lax.dot_general(query, keys[i], (((1,), (1,)), ((), ())), preferred_element_type=jnp.float32) * scale
        position = mp * (places // kv_heads) + lanes // kv_heads
        valid = position < lengths[i]
        weights, tops, totals, added = [], [], [], []
        for b in range(kv_heads):
            span = slice(b * per_group, (b + 1) * per_group)
            allowed = valid & (lanes % kv_heads == b)
            mine = jnp.sum(query[span].astype(jnp.float32) * fresh[b : b + 1], axis=1, keepdims=True) * scale
            mine = jnp.where(mp == 0, mine, -1e30)
            top = jnp.max(jnp.where(allowed, scores[span], -1e30), axis=1, keepdims=True)
            top = jnp.maximum(top, mine)
            probable = jnp.where(allowed, jnp.exp(scores[span] - top), 0.0)
            own = jnp.where(mp == 0, jnp.exp(mine - top), 0.0)
            total = jnp.sum(probable, axis=1, keepdims=True) + own
            weights.append(probable)
            added.append(own * fresh[kv_heads + b : kv_heads + b + 1])
            stats[b] = jnp.where(stats_lane == 2 * i, top, stats[b])
            stats[b] = jnp.where(stats_lane == 2 * i + 1, total, stats[b])
        weight = jnp.concatenate(weights, axis=0).astype(jnp.bfloat16)
        out = jnp.dot(weight, values[i], preferred_element_type=jnp.float32) + jnp.concatenate(added, axis=0)
        for m in range(n_mp):
            packed[m, i * heads_here : (i + 1) * heads_here, :] = out[m * heads_here : (m + 1) * heads_here]
    for m in range(n_mp):
        here = jnp.concatenate(stats[m * heads_here // per_group : (m + 1) * heads_here // per_group], axis=0)
        packed[m, rows_here * heads_here :, :] = here
    for k, ref in enumerate(outs):
        ref[...] = packed[jnp.bitwise_xor(mp, k)]


def join_kernel(*refs):
    parts, out = refs[:-1], refs[-1]
    rows_here, heads_here, head_size = out.shape
    step = LANES // (2 * rows_here)
    stats = rows_here * heads_here
    for i in range(rows_here):
        tops = [p[stats:, 2 * i * step : 2 * i * step + 1] for p in parts]
        sums = [p[stats:, (2 * i + 1) * step : (2 * i + 1) * step + 1] for p in parts]
        joined = functools.reduce(jnp.maximum, tops)
        scales = [jnp.exp(top - joined) for top in tops]
        numerator = sum(p[i * heads_here : (i + 1) * heads_here, :] * s for p, s in zip(parts, scales))
        divisor = sum(n * s for n, s in zip(sums, scales))
        out[i] = (numerator / divisor).astype(out.dtype)


def exchanged(value, axis, count):
    return [value] + [lax.ppermute(value, axis, [(i, i ^ k) for i in range(count)]) for k in range(1, count)]


def close(
    sizes, inputs, stale_rows, row_order, lengths, old_q, old_kv, fresh_q, fresh_kv, key_cache, value_cache
):
    n_grp, n_rep, n_mp = sizes
    group_rows, part_width = inputs.shape
    heads_here = old_q.shape[1]
    head_size = old_q.shape[2]
    slice_here = fresh_q.shape[2]
    rows = group_rows * n_grp
    rows_here, positions_here, kv_heads, _ = key_cache.shape
    shares = heads_here // n_grp
    parts = shares + 1
    bf16 = functools.partial(jax.ShapeDtypeStruct, dtype=jnp.bfloat16)
    f32 = functools.partial(jax.ShapeDtypeStruct, dtype=jnp.float32)
    moved = pl.pallas_call(
        order_kernel,
        out_shape=bf16((group_rows, part_width + LANES)),
        in_specs=[whole_block(HBM)] * 4,
        out_specs=whole_block(VMEM),
        scratch_shapes=[
            pltpu.SMEM((group_rows,), jnp.int32),
            pltpu.SMEM((group_rows,), jnp.int32),
            pltpu.VMEM((group_rows, part_width), jnp.bfloat16),
            pltpu.SemaphoreType.DMA((3,)),
        ],
        compiler_params=pltpu.CompilerParams(vmem_limit_bytes=ROOMY),
        cost_estimate=pl.CostEstimate(flops=0, bytes_accessed=START_BYTES, transcendentals=0),
        name="order",
    )(row_order, stale_rows, inputs, old_q)
    gathered = exchanged(moved, "grp", n_grp)
    near = (
        old_kv.reshape(part_width * n_grp, head_size),
        jnp.transpose(fresh_q, (1, 2, 0)).reshape(heads_here * slice_here, part_width),
        jnp.transpose(fresh_kv, (1, 2, 0)).reshape(n_grp * slice_here, part_width),
    )
    near_q = pl.pallas_call(
        load_kernel,
        out_shape=bf16((part_width, shares, head_size)),
        in_specs=[whole_block(HBM)] + [whole_block(VMEM)] * 3,
        out_specs=whole_block(pl.ANY),
        scratch_shapes=[pltpu.SemaphoreType.DMA],
        compiler_params=pltpu.CompilerParams(vmem_limit_bytes=LOAD_LIMIT),
        name="load",
    )(old_q.reshape(part_width, n_grp, shares, head_size), *near)
    block = n_mp * rows_here * parts
    terms = pl.pallas_call(
        functools.partial(project_kernel, n_rep, n_mp),
        out_shape=f32((n_grp * n_rep, block, head_size)),
        in_specs=[whole_block(VMEM)] * (n_grp + 4),
        out_specs=whole_block(VMEM),
        scratch_shapes=[
            pltpu.VMEM((rows, part_width + LANES), jnp.bfloat16),
            pltpu.VMEM((rows * parts, LANES), jnp.float32),
        ],
        compiler_params=pltpu.CompilerParams(vmem_limit_bytes=PROJECT_LIMIT),
        name="project",
    )(*gathered, near_q.reshape(part_width * shares, head_size), *near)
    devices = n_grp * n_rep * n_mp
    held = lax.all_to_all(terms.reshape(devices, 1, rows_here * parts * head_size), AXES, 0, 0, tiled=True)
    held = held.reshape(n_grp * n_rep, block, head_size)
    places = positions_here * kv_heads
    packed_rows = (rows_here + 1) * heads_here
    partial_out = pl.pallas_call(
        functools.partial(attend_kernel, sizes, 1.0 / math.sqrt(head_size)),
        out_shape=[f32((packed_rows, LANES))] * n_mp,
        in_specs=[whole_block(SMEM)] * 3 + [whole_block(VMEM)] * 3,
        out_specs=[whole_block(VMEM)] * n_mp,
        scratch_shapes=[
            pltpu.VMEM((n_grp * block, LANES), jnp.float32),
            pltpu.VMEM((n_grp * block, LANES), jnp.float32),
            pltpu.VMEM((rows_here * heads_here * n_mp, LANES), jnp.float32),
            pltpu.VMEM((rows_here * 2 * kv_heads, LANES), jnp.float32),
            pltpu.VMEM((n_mp, packed_rows, LANES), jnp.float32),
        ],
        compiler_params=pltpu.CompilerParams(vmem_limit_bytes=16 << 20),
        name="attend",
    )(
        row_order,
        stale_rows,
        lengths,
        held,
        key_cache.reshape(rows_here, places, head_size),
        value_cache.reshape(rows_here, places, head_size),
    )
    pieces = [partial_out[0]] + [
        lax.ppermute(partial_out[k], "mp", [(i, i ^ k) for i in range(n_mp)]) for k in range(n_mp - 1, 0, -1)
    ]
    return pl.pallas_call(
        join_kernel,
        out_shape=bf16((rows_here, heads_here, head_size)),
        in_specs=[whole_block(VMEM)] * n_mp,
        out_specs=whole_block(VMEM),
        compiler_params=pltpu.CompilerParams(vmem_limit_bytes=4 << 20),
        name="join",
    )(*pieces)


def fits(sizes, old_q, old_kv, fresh_q, key_cache):
    n_grp, n_rep, n_mp = sizes
    heads_here, head_size = old_q.shape[1:]
    slots_here = old_kv.shape[1]
    rows_here, _, kv_heads, _ = key_cache.shape
    return (
        head_size == LANES
        and slots_here == n_grp
        and heads_here == n_grp * n_grp
        and fresh_q.shape[2] * n_grp == head_size
        and n_grp & (n_grp - 1) == 0
        and n_mp & (n_mp - 1) == 0
        and heads_here * n_mp == SUBLANES * kv_heads
        and heads_here % SUBLANES == 0
        and slots_here * n_mp == 2 * kv_heads
        and n_mp * rows_here * (n_grp + 1) % SUBLANES == 0
        and LANES % (2 * rows_here) == 0
        and n_grp * n_rep * rows_here % (2 * SUBLANES) == 0
        and old_q.shape[0] % (2 * SPANS * LANES) == 0
    )


def local(sizes, *args):
    old_q, old_kv, fresh_q, key_cache = args[4], args[5], args[6], args[8]
    return (close if fits(sizes, old_q, old_kv, fresh_q, key_cache) else plain)(sizes, *args)


def solution(mesh):
    sizes = tuple(mesh.shape[a] for a in AXES)
    return jax.shard_map(
        functools.partial(local, sizes),
        mesh=mesh,
        in_specs=(
            P("grp", "rep"),
            P("grp"),
            P("grp"),
            P(("grp", "rep")),
            P("rep", "mp", None),
            P("rep", "mp", None),
            P("rep", "mp", "grp"),
            P("rep", "mp", "grp"),
            P(("grp", "rep"), "mp", None, None),
            P(("grp", "rep"), "mp", None, None),
        ),
        out_specs=P(("grp", "rep"), "mp", None),
        check_vma=False,
    )
```

```python
import functools
import math

import jax
import jax.numpy as jnp
from jax import lax
from jax.experimental import pallas as pl
from jax.experimental.pallas import tpu as pltpu
from jax.sharding import PartitionSpec as P

AXES = ("grp", "rep", "mp")


def slot_order(inputs, stale_rows, row_order):
    lanes = 128
    flags = jnp.broadcast_to(stale_rows.astype(inputs.dtype)[:, None], (inputs.shape[0], lanes))
    rows = jnp.concatenate([inputs, flags], axis=1)
    slots = jnp.arange(inputs.shape[0], dtype=row_order.dtype)
    moved = 0
    for i in range(inputs.shape[0]):
        moved = moved + jnp.where((slots == row_order[i])[:, None], rows[i][None], 0)
    return moved


def plain(
    sizes, inputs, stale_rows, row_order, lengths, old_q, old_kv, fresh_q, fresh_kv, key_cache, value_cache
):
    n_grp, n_rep, n_mp = sizes
    part_width = inputs.shape[1]
    heads_here = old_q.shape[1]
    head_size = old_q.shape[2]
    slice_here = fresh_q.shape[2]
    slots_here = heads_here + old_kv.shape[1]
    gathered = lax.all_gather(slot_order(inputs, stale_rows, row_order), "grp", axis=0, tiled=True)
    rows_all = gathered.shape[0]
    features = gathered[:, :part_width]
    stale = gathered[:, part_width] == 1
    first = lax.axis_index("grp") * slice_here

    def project(q, kv):
        parts = [jnp.einsum("bf,fhd->bhd", features, w, preferred_element_type=jnp.float32) for w in (q, kv)]
        return jnp.concatenate(parts, axis=1)

    cut = functools.partial(lax.dynamic_slice_in_dim, start_index=first, slice_size=slice_here, axis=2)
    terms = jnp.where(stale[:, None, None], project(cut(old_q), cut(old_kv)), project(fresh_q, fresh_kv))
    rows_here = rows_all // (n_grp * n_rep)
    terms = terms.reshape(n_grp * n_rep, 1, rows_here * slots_here * slice_here)
    terms = jnp.broadcast_to(terms, (n_grp * n_rep, n_mp, terms.shape[2]))
    terms = terms.reshape(n_grp * n_rep * n_mp, 1, terms.shape[2])
    held = lax.all_to_all(terms, AXES, 0, 0, tiled=True)
    held = held.reshape(n_grp, n_rep, n_mp, rows_here, slots_here, slice_here)
    held = jnp.sum(held, axis=1).astype(jnp.bfloat16)
    held = jnp.transpose(held, (2, 1, 3, 0, 4)).reshape(rows_here, n_mp, slots_here, head_size)
    queries = held[:, :, :heads_here].reshape(rows_here, n_mp * heads_here, head_size)
    slots = held[:, :, heads_here:].reshape(rows_here, -1, head_size)
    kv_heads = slots.shape[1] // 2
    head_count = queries.shape[1]
    per_group = head_count // kv_heads
    scale = 1.0 / math.sqrt(head_size)
    grouped = queries.reshape(rows_here, kv_heads, per_group, head_size)
    scores = jnp.einsum("bkgd,blkd->bkgl", grouped, key_cache, preferred_element_type=jnp.float32) * scale
    positions_here = key_cache.shape[1]
    positions = lax.axis_index("mp") * positions_here + jnp.arange(positions_here, dtype=jnp.int32)
    allowed = (positions[None, :] < lengths[:, None])[:, None, None, :]
    new_keys = slots[:, :kv_heads, None].astype(jnp.float32)
    new_values = slots[:, kv_heads:, None].astype(jnp.float32)
    new_score = jnp.sum(grouped.astype(jnp.float32) * new_keys, axis=-1) * scale
    new_score = jnp.where(lax.axis_index("mp") == 0, new_score, -1e30)
    top = jnp.maximum(jnp.max(jnp.where(allowed, scores, -1e30), axis=-1), new_score)
    probable = jnp.where(allowed, jnp.exp(scores - top[..., None]), 0.0)
    new_weight = jnp.where(lax.axis_index("mp") == 0, jnp.exp(new_score - top), 0.0)
    total = jnp.sum(probable, axis=-1) + new_weight
    out = jnp.einsum("bkgl,blkd->bkgd", probable.astype(jnp.bfloat16), value_cache, preferred_element_type=jnp.float32)
    out = out + new_weight[..., None] * new_values
    flat = (rows_here, head_count)
    part = jnp.concatenate(
        [out.reshape(*flat, head_size), top.reshape(*flat, 1), total.reshape(*flat, 1)], axis=2
    )
    part = lax.all_to_all(part[None], "mp", split_axis=2, concat_axis=0, tiled=True)
    outs, tops, totals = part[..., :head_size], part[..., head_size], part[..., head_size + 1]
    weights = jnp.exp(tops - jnp.max(tops, axis=0)[None])
    numerator = jnp.sum(outs * weights[..., None], axis=0)
    return (numerator / jnp.sum(totals * weights, axis=0)[..., None]).astype(jnp.bfloat16)


LANES = 128
SUBLANES = 8
HBM = pltpu.MemorySpace.HBM
VMEM = pltpu.MemorySpace.VMEM
SMEM = pltpu.MemorySpace.SMEM
ROOMY = 57000000
LOAD_LIMIT = 40_000_000
PROJECT_LIMIT = 24_000_000
START_BYTES = 32 << 20
SPANS = 4
NEVER = -1e30


def whole_block(space):
    return pl.BlockSpec(memory_space=space)


def order_kernel(order_in, stale_in, rows_in, _, moved, order, stale, rows, sems):
    pairs = ((order_in, order), (stale_in, stale), (rows_in, rows))
    copies = [pltpu.make_async_copy(a, b, sems.at[n]) for n, (a, b) in enumerate(pairs)]
    for copy in copies:
        copy.start()
    for copy in copies:
        copy.wait()
    count, width = rows.shape
    where_row = lax.broadcasted_iota(jnp.int32, (count, 1), 0)
    total = jnp.zeros((count, width), jnp.float32)
    flags = jnp.zeros((count, LANES), jnp.float32)
    for i in range(count):
        here = where_row == order[i]
        total = jnp.where(here, rows[i : i + 1, :].astype(jnp.float32), total)
        flags = jnp.where(here, stale[i].astype(jnp.float32), flags)
    moved[:, :width] = total.astype(moved.dtype)
    moved[:, width:] = flags.astype(moved.dtype)


def load_kernel(old_q, *refs):
    near, sem = refs[-2:]
    copy = pltpu.make_async_copy(old_q.at[:, lax.axis_index("grp")], near, sem)
    copy.start()
    copy.wait()


def project_kernel(n_rep, n_mp, *refs):
    rows_in = refs[:-7]
    old_q, old_kv, fresh_q, fresh_kv, out, features, staged = refs[-7:]
    n_grp = len(rows_in)
    mine = lax.axis_index("grp")
    group_rows, width = rows_in[0].shape
    rows = group_rows * n_grp
    part_width = width - LANES
    per_row = old_q.shape[0] // part_width
    for k, part in enumerate(rows_in):
        features[k * group_rows : (k + 1) * group_rows, :] = part[...]
    chunks = part_width // LANES
    stacked = jnp.concatenate([features[:, c * LANES : (c + 1) * LANES] for c in range(chunks)], axis=0)
    spread_width = LANES * per_row
    source = lax.broadcasted_iota(jnp.int32, (LANES, spread_width), 0)
    target = lax.broadcasted_iota(jnp.int32, (LANES, spread_width), 1)
    spread = jnp.where(target // per_row == source, 1.0, 0.0).astype(jnp.bfloat16)
    wide = jnp.dot(stacked, spread, preferred_element_type=jnp.float32).astype(jnp.bfloat16)
    lane = lax.broadcasted_iota(jnp.int32, (1, spread_width), 1) % per_row
    picks = [jnp.where(lane == h, 1.0, 0.0).astype(jnp.bfloat16) for h in range(per_row)]

    def add(weights):
        half = chunks // 2
        sums = []
        for side in range(2):
            total = 0
            for c in range(side * half, (side + 1) * half, SPANS):
                left = []
                for u in range(c, c + SPANS):
                    piece = wide[u * rows : (u + 1) * rows]
                    left.append(jnp.concatenate([piece * pick for pick in picks], axis=0))
                left = jnp.concatenate(left, axis=1)
                right = weights[c * spread_width : (c + SPANS) * spread_width, :]
                total = total + jnp.dot(left, right, preferred_element_type=jnp.float32)
            sums.append(total)
        return sums[0] + sums[1]

    across = (((1,), (1,)), ((), ()))
    kept_kv = add(old_kv)
    values = features[:, :part_width]
    new_q = lax.dot_general(fresh_q[...], values, across, preferred_element_type=jnp.float32).T
    new_kv = lax.dot_general(fresh_kv[...], values, across, preferred_element_type=jnp.float32).T
    kept_q = add(old_q)
    stale = features[:, part_width : part_width + 1].astype(jnp.float32) == 1.0
    for j in range(per_row):
        span = slice(j * LANES, (j + 1) * LANES)
        staged[j * rows : (j + 1) * rows, :] = jnp.where(stale, kept_q[j * rows : (j + 1) * rows], new_q[:, span])
    kept = kept_kv[:rows]
    for h in range(1, per_row):
        kept = jnp.where(mine == h, kept_kv[h * rows : (h + 1) * rows], kept)
    staged[per_row * rows :, :] = jnp.where(stale, kept, new_kv)
    parts = per_row + 1
    rows_here = group_rows // n_rep
    for k in range(n_grp):
        group = jnp.bitwise_xor(mine, k)
        for r in range(n_rep):
            for i in range(rows_here):
                row = k * group_rows + r * rows_here + i
                block = staged[pl.ds(row, parts, stride=rows), :]
                for m in range(n_mp):
                    first = (m * rows_here + i) * parts
                    out[group * n_rep + r, first : first + parts, :] = block


def attend_kernel(sizes, scale, order, stale, lengths, held, keys, values, *refs):
    n_grp, n_rep, n_mp = sizes
    outs = refs[:n_mp]
    summed, turned, queries, slots, packed = refs[n_mp:]
    rows_here, places, head_size = keys.shape
    slots_here = n_grp
    heads_here = queries.shape[0] // (rows_here * n_mp)
    head_count = heads_here * n_mp
    kv_heads = slots_here * n_mp // 2
    per_group = head_count // kv_heads
    shares = heads_here // n_grp
    parts = shares + 1
    block = held.shape[1]
    step = head_size // n_grp
    mp = lax.axis_index("mp")
    rep = lax.axis_index("rep")
    sums = []
    for g in range(n_grp):
        total = held[g * n_rep]
        for r in range(1, n_rep):
            total = total + held[g * n_rep + r]
        sums.append(total)
        summed[g * block : (g + 1) * block, :] = total
    lane = lax.broadcasted_iota(jnp.int32, (1, head_size), 1) // step
    for h in range(n_grp):
        total = sums[h]
        for g in range(n_grp):
            if g != h:
                total = jnp.where(lane == g, pltpu.roll(sums[g], (step * (g - h)) % head_size, 1), total)
        turned[h * block : (h + 1) * block, :] = total
    lanes = lax.broadcasted_iota(jnp.int32, (SUBLANES, places), 1)
    head_of = lanes % kv_heads
    place_of = mp * (places // kv_heads) + lanes // kv_heads
    fields = 2 * rows_here
    stats_lane = lax.broadcasted_iota(jnp.int32, (1, LANES), 1) // (LANES // fields)
    stats = [jnp.zeros((per_group, LANES), jnp.float32) for _ in range(kv_heads)]
    for i in range(rows_here):
        flag = jnp.int32(0)
        for n in range(order.shape[0]):
            flag = jnp.where(order[n] == rep * rows_here + i, stale[n], flag)

        @pl.when(flag == 1)
        def _():
            for m in range(n_mp):
                base = (m * rows_here + i) * parts
                for g in range(n_grp):
                    first = i * head_count + m * heads_here + g * shares
                    queries[first : first + shares, :] = summed[g * block + base : g * block + base + shares, :]
                first = i * n_mp * slots_here + m * slots_here
                slots[first : first + slots_here, :] = summed[pl.ds(base + shares, slots_here, stride=block), :]

        @pl.when(flag != 1)
        def _():
            for m in range(n_mp):
                base = (m * rows_here + i) * parts
                for j in range(shares):
                    first = i * head_count + m * heads_here + j * n_grp
                    queries[first : first + n_grp, :] = turned[pl.ds(base + j, n_grp, stride=block), :]
                first = i * n_mp * slots_here + m * slots_here
                slots[first : first + slots_here, :] = turned[pl.ds(base + shares, slots_here, stride=block), :]

        query = queries[i * head_count : (i + 1) * head_count, :].astype(jnp.bfloat16)
        fresh = slots[i * 2 * kv_heads : (i + 1) * 2 * kv_heads, :].astype(jnp.bfloat16).astype(jnp.float32)
        scores = lax.dot_general(query, keys[i], (((1,), (1,)), ((), ())), preferred_element_type=jnp.float32)
        head_here = jnp.where(place_of < lengths[i], head_of, -1)
        weights, added = [], []
        for b in range(kv_heads):
            span = slice(b * per_group, (b + 1) * per_group)
            mine = jnp.sum(query[span].astype(jnp.float32) * fresh[b : b + 1], axis=1, keepdims=True)
            mine = jnp.where(mp == 0, mine, NEVER)
            held_scores = jnp.where(head_here == b, scores[span], NEVER)
            top = jnp.maximum(jnp.max(held_scores, axis=1, keepdims=True), mine)
            base = jnp.where(top == NEVER, 0.0, top)
            probable = jnp.exp2((held_scores - base) * scale)
            own = jnp.exp2((mine - base) * scale)
            total = jnp.sum(probable, axis=1, keepdims=True) + own
            weights.append(probable)
            added.append(own * fresh[kv_heads + b : kv_heads + b + 1])
            for n, value in enumerate((top, total)):
                stats[b] = jnp.where(stats_lane == 2 * i + n, value, stats[b])
        weight = jnp.concatenate(weights, axis=0).astype(jnp.bfloat16)
        out = jnp.dot(weight, values[i], preferred_element_type=jnp.float32) + jnp.concatenate(added, axis=0)
        for m in range(n_mp):
            packed[m, i * heads_here : (i + 1) * heads_here, :] = out[m * heads_here : (m + 1) * heads_here]
    for m in range(n_mp):
        here = jnp.concatenate(stats[m * heads_here // per_group : (m + 1) * heads_here // per_group], axis=0)
        packed[m, rows_here * heads_here :, :] = here
    for k, ref in enumerate(outs):
        ref[...] = packed[jnp.bitwise_xor(mp, k)]


def join_kernel(scale, *refs):
    parts, out = refs[:-1], refs[-1]
    rows_here, heads_here, head_size = out.shape
    step = LANES // (2 * rows_here)
    values = [p[...] for p in parts]
    stats = [v[rows_here * heads_here :, :] for v in values]

    def field(block, n):
        return block[:, n * step : n * step + 1]

    for i in range(rows_here):
        tops = [field(block, 2 * i) for block in stats]
        joined = functools.reduce(jnp.maximum, tops)
        scales = [jnp.exp2((top - joined) * scale) for top in tops]
        numerator = sum(v[i * heads_here : (i + 1) * heads_here, :] * s for v, s in zip(values, scales))
        divisor = sum(field(block, 2 * i + 1) * s for block, s in zip(stats, scales))
        out[i] = (numerator / divisor).astype(out.dtype)


def exchanged(value, axis, count):
    return [value] + [lax.ppermute(value, axis, [(i, i ^ k) for i in range(count)]) for k in range(1, count)]


def close(
    sizes, inputs, stale_rows, row_order, lengths, old_q, old_kv, fresh_q, fresh_kv, key_cache, value_cache
):
    n_grp, n_rep, n_mp = sizes
    group_rows, part_width = inputs.shape
    heads_here = old_q.shape[1]
    head_size = old_q.shape[2]
    slice_here = fresh_q.shape[2]
    rows = group_rows * n_grp
    rows_here, positions_here, kv_heads, _ = key_cache.shape
    shares = heads_here // n_grp
    parts = shares + 1
    bf16 = functools.partial(jax.ShapeDtypeStruct, dtype=jnp.bfloat16)
    f32 = functools.partial(jax.ShapeDtypeStruct, dtype=jnp.float32)
    moved = pl.pallas_call(
        order_kernel,
        out_shape=bf16((group_rows, part_width + LANES)),
        in_specs=[whole_block(HBM)] * 4,
        out_specs=whole_block(VMEM),
        scratch_shapes=[
            pltpu.SMEM((group_rows,), jnp.int32),
            pltpu.SMEM((group_rows,), jnp.int32),
            pltpu.VMEM((group_rows, part_width), jnp.bfloat16),
            pltpu.SemaphoreType.DMA((3,)),
        ],
        compiler_params=pltpu.CompilerParams(vmem_limit_bytes=ROOMY),
        cost_estimate=pl.CostEstimate(flops=0, bytes_accessed=START_BYTES, transcendentals=0),
        name="order",
    )(row_order, stale_rows, inputs, old_q)
    gathered = exchanged(moved, "grp", n_grp)
    near = (
        old_kv.reshape(part_width * n_grp, head_size),
        jnp.transpose(fresh_q, (1, 2, 0)).reshape(heads_here * slice_here, part_width),
        jnp.transpose(fresh_kv, (1, 2, 0)).reshape(n_grp * slice_here, part_width),
    )
    near_q = pl.pallas_call(
        load_kernel,
        out_shape=bf16((part_width, shares, head_size)),
        in_specs=[whole_block(HBM)] + [whole_block(VMEM)] * 3,
        out_specs=whole_block(pl.ANY),
        scratch_shapes=[pltpu.SemaphoreType.DMA],
        compiler_params=pltpu.CompilerParams(vmem_limit_bytes=LOAD_LIMIT),
        name="load",
    )(old_q.reshape(part_width, n_grp, shares, head_size), *near)
    block = n_mp * rows_here * parts
    terms = pl.pallas_call(
        functools.partial(project_kernel, n_rep, n_mp),
        out_shape=f32((n_grp * n_rep, block, head_size)),
        in_specs=[whole_block(VMEM)] * (n_grp + 4),
        out_specs=whole_block(VMEM),
        scratch_shapes=[
            pltpu.VMEM((rows, part_width + LANES), jnp.bfloat16),
            pltpu.VMEM((rows * parts, LANES), jnp.float32),
        ],
        compiler_params=pltpu.CompilerParams(vmem_limit_bytes=PROJECT_LIMIT),
        name="project",
    )(*gathered, near_q.reshape(part_width * shares, head_size), *near)
    devices = n_grp * n_rep * n_mp
    held = lax.all_to_all(terms.reshape(devices, 1, rows_here * parts * head_size), AXES, 0, 0, tiled=True)
    held = held.reshape(n_grp * n_rep, block, head_size)
    places = positions_here * kv_heads
    packed_rows = (rows_here + 1) * heads_here
    scale = math.log2(math.e) / math.sqrt(head_size)
    partial_out = pl.pallas_call(
        functools.partial(attend_kernel, sizes, scale),
        out_shape=[f32((packed_rows, LANES))] * n_mp,
        in_specs=[whole_block(SMEM)] * 3 + [whole_block(VMEM)] * 3,
        out_specs=[whole_block(VMEM)] * n_mp,
        scratch_shapes=[
            pltpu.VMEM((n_grp * block, LANES), jnp.float32),
            pltpu.VMEM((n_grp * block, LANES), jnp.float32),
            pltpu.VMEM((rows_here * heads_here * n_mp, LANES), jnp.float32),
            pltpu.VMEM((rows_here * 2 * kv_heads, LANES), jnp.float32),
            pltpu.VMEM((n_mp, packed_rows, LANES), jnp.float32),
        ],
        compiler_params=pltpu.CompilerParams(vmem_limit_bytes=16 << 20),
        name="attend",
    )(
        row_order,
        stale_rows,
        lengths,
        held,
        key_cache.reshape(rows_here, places, head_size),
        value_cache.reshape(rows_here, places, head_size),
    )
    pieces = [partial_out[0]] + [
        lax.ppermute(partial_out[k], "mp", [(i, i ^ k) for i in range(n_mp)]) for k in range(n_mp - 1, 0, -1)
    ]
    return pl.pallas_call(
        functools.partial(join_kernel, scale),
        out_shape=bf16((rows_here, heads_here, head_size)),
        in_specs=[whole_block(VMEM)] * n_mp,
        out_specs=whole_block(VMEM),
        compiler_params=pltpu.CompilerParams(vmem_limit_bytes=4 << 20),
        name="join",
    )(*pieces)


def fits(sizes, old_q, old_kv, fresh_q, key_cache):
    n_grp, n_rep, n_mp = sizes
    heads_here, head_size = old_q.shape[1:]
    slots_here = old_kv.shape[1]
    rows_here, _, kv_heads, _ = key_cache.shape
    return (
        head_size == LANES
        and slots_here == n_grp
        and heads_here == n_grp * n_grp
        and fresh_q.shape[2] * n_grp == head_size
        and n_grp & (n_grp - 1) == 0
        and n_mp & (n_mp - 1) == 0
        and heads_here * n_mp == SUBLANES * kv_heads
        and heads_here % SUBLANES == 0
        and slots_here * n_mp == 2 * kv_heads
        and n_mp * rows_here * (n_grp + 1) % SUBLANES == 0
        and LANES // (2 * rows_here) > 0
        and n_grp * n_rep * rows_here % (2 * SUBLANES) == 0
        and old_q.shape[0] % (2 * SPANS * LANES) == 0
    )


def local(sizes, *args):
    old_q, old_kv, fresh_q, key_cache = args[4], args[5], args[6], args[8]
    return (close if fits(sizes, old_q, old_kv, fresh_q, key_cache) else plain)(sizes, *args)


def solution(mesh):
    sizes = tuple(mesh.shape[a] for a in AXES)
    return jax.shard_map(
        functools.partial(local, sizes),
        mesh=mesh,
        in_specs=(
            P("grp", "rep"),
            P("grp"),
            P("grp"),
            P(("grp", "rep")),
            P("rep", "mp", None),
            P("rep", "mp", None),
            P("rep", "mp", "grp"),
            P("rep", "mp", "grp"),
            P(("grp", "rep"), "mp", None, None),
            P(("grp", "rep"), "mp", None, None),
        ),
        out_specs=P(("grp", "rep"), "mp", None),
        check_vma=False,
    )
```

```python
import functools
import math

import jax
import jax.numpy as jnp
from jax import lax
from jax.experimental import pallas as pl
from jax.experimental.pallas import tpu as pltpu
from jax.sharding import PartitionSpec as P

AXES = ("grp", "rep", "mp")


def slot_order(inputs, stale_rows, row_order):
    lanes = 128
    flags = jnp.broadcast_to(stale_rows.astype(inputs.dtype)[:, None], (inputs.shape[0], lanes))
    rows = jnp.concatenate([inputs, flags], axis=1)
    slots = jnp.arange(inputs.shape[0], dtype=row_order.dtype)
    moved = 0
    for i in range(inputs.shape[0]):
        moved = moved + jnp.where((slots == row_order[i])[:, None], rows[i][None], 0)
    return moved


def plain(
    sizes, inputs, stale_rows, row_order, lengths, old_q, old_kv, fresh_q, fresh_kv, key_cache, value_cache
):
    n_grp, n_rep, n_mp = sizes
    part_width = inputs.shape[1]
    heads_here = old_q.shape[1]
    head_size = old_q.shape[2]
    slice_here = fresh_q.shape[2]
    slots_here = heads_here + old_kv.shape[1]
    gathered = lax.all_gather(slot_order(inputs, stale_rows, row_order), "grp", axis=0, tiled=True)
    rows_all = gathered.shape[0]
    features = gathered[:, :part_width]
    stale = gathered[:, part_width] == 1
    first = lax.axis_index("grp") * slice_here

    def project(q, kv):
        parts = [jnp.einsum("bf,fhd->bhd", features, w, preferred_element_type=jnp.float32) for w in (q, kv)]
        return jnp.concatenate(parts, axis=1)

    cut = functools.partial(lax.dynamic_slice_in_dim, start_index=first, slice_size=slice_here, axis=2)
    terms = jnp.where(stale[:, None, None], project(cut(old_q), cut(old_kv)), project(fresh_q, fresh_kv))
    rows_here = rows_all // (n_grp * n_rep)
    terms = terms.reshape(n_grp * n_rep, 1, rows_here * slots_here * slice_here)
    terms = jnp.broadcast_to(terms, (n_grp * n_rep, n_mp, terms.shape[2]))
    terms = terms.reshape(n_grp * n_rep * n_mp, 1, terms.shape[2])
    held = lax.all_to_all(terms, AXES, 0, 0, tiled=True)
    held = held.reshape(n_grp, n_rep, n_mp, rows_here, slots_here, slice_here)
    held = jnp.sum(held, axis=1).astype(jnp.bfloat16)
    held = jnp.transpose(held, (2, 1, 3, 0, 4)).reshape(rows_here, n_mp, slots_here, head_size)
    queries = held[:, :, :heads_here].reshape(rows_here, n_mp * heads_here, head_size)
    slots = held[:, :, heads_here:].reshape(rows_here, -1, head_size)
    kv_heads = slots.shape[1] // 2
    head_count = queries.shape[1]
    per_group = head_count // kv_heads
    scale = 1.0 / math.sqrt(head_size)
    grouped = queries.reshape(rows_here, kv_heads, per_group, head_size)
    scores = jnp.einsum("bkgd,blkd->bkgl", grouped, key_cache, preferred_element_type=jnp.float32) * scale
    positions_here = key_cache.shape[1]
    positions = lax.axis_index("mp") * positions_here + jnp.arange(positions_here, dtype=jnp.int32)
    allowed = (positions[None, :] < lengths[:, None])[:, None, None, :]
    new_keys = slots[:, :kv_heads, None].astype(jnp.float32)
    new_values = slots[:, kv_heads:, None].astype(jnp.float32)
    new_score = jnp.sum(grouped.astype(jnp.float32) * new_keys, axis=-1) * scale
    new_score = jnp.where(lax.axis_index("mp") == 0, new_score, -1e30)
    top = jnp.maximum(jnp.max(jnp.where(allowed, scores, -1e30), axis=-1), new_score)
    probable = jnp.where(allowed, jnp.exp(scores - top[..., None]), 0.0)
    new_weight = jnp.where(lax.axis_index("mp") == 0, jnp.exp(new_score - top), 0.0)
    total = jnp.sum(probable, axis=-1) + new_weight
    out = jnp.einsum("bkgl,blkd->bkgd", probable.astype(jnp.bfloat16), value_cache, preferred_element_type=jnp.float32)
    out = out + new_weight[..., None] * new_values
    flat = (rows_here, head_count)
    part = jnp.concatenate(
        [out.reshape(*flat, head_size), top.reshape(*flat, 1), total.reshape(*flat, 1)], axis=2
    )
    part = lax.all_to_all(part[None], "mp", split_axis=2, concat_axis=0, tiled=True)
    outs, tops, totals = part[..., :head_size], part[..., head_size], part[..., head_size + 1]
    weights = jnp.exp(tops - jnp.max(tops, axis=0)[None])
    numerator = jnp.sum(outs * weights[..., None], axis=0)
    return (numerator / jnp.sum(totals * weights, axis=0)[..., None]).astype(jnp.bfloat16)


LANES = 128
SUBLANES = 8
HBM = pltpu.MemorySpace.HBM
VMEM = pltpu.MemorySpace.VMEM
SMEM = pltpu.MemorySpace.SMEM
ROOMY = 57000000
LOAD_LIMIT = 40_000_000
PROJECT_LIMIT = 24_000_000
START_BYTES = 32 << 20
SPANS = 16
NEVER = -1e30


def whole_block(space):
    return pl.BlockSpec(memory_space=space)


def order_kernel(order_in, stale_in, rows_in, _, moved, order, stale, rows, sems):
    pairs = ((order_in, order), (stale_in, stale), (rows_in, rows))
    copies = [pltpu.make_async_copy(a, b, sems.at[n]) for n, (a, b) in enumerate(pairs)]
    for copy in copies:
        copy.start()
    for copy in copies:
        copy.wait()
    count, width = rows.shape
    where_row = lax.broadcasted_iota(jnp.int32, (count, 1), 0)
    total = jnp.zeros((count, width), jnp.float32)
    flags = jnp.zeros((count, LANES), jnp.float32)
    for i in range(count):
        here = where_row == order[i]
        total = jnp.where(here, rows[i : i + 1, :].astype(jnp.float32), total)
        flags = jnp.where(here, stale[i].astype(jnp.float32), flags)
    moved[:, :width] = total.astype(moved.dtype)
    moved[:, width:] = flags.astype(moved.dtype)


def load_kernel(old_q, *refs):
    near, sem = refs[-2:]
    copy = pltpu.make_async_copy(old_q.at[:, lax.axis_index("grp")], near, sem)
    copy.start()
    copy.wait()


def project_kernel(n_rep, n_mp, *refs):
    rows_in = refs[:-7]
    old_q, old_kv, fresh_q, fresh_kv, out, features, staged = refs[-7:]
    n_grp = len(rows_in)
    mine = lax.axis_index("grp")
    group_rows, width = rows_in[0].shape
    rows = group_rows * n_grp
    part_width = width - LANES
    per_row = old_q.shape[0] // part_width
    for k, part in enumerate(rows_in):
        features[k * group_rows : (k + 1) * group_rows, :] = part[...]
    chunks = part_width // LANES
    stacked = jnp.concatenate([features[:, c * LANES : (c + 1) * LANES] for c in range(chunks)], axis=0)
    spread_width = LANES * per_row
    source = lax.broadcasted_iota(jnp.int32, (LANES, spread_width), 0)
    target = lax.broadcasted_iota(jnp.int32, (LANES, spread_width), 1)
    spread = jnp.where(target // per_row == source, 1.0, 0.0).astype(jnp.bfloat16)
    wide = jnp.dot(stacked, spread, preferred_element_type=jnp.float32).astype(jnp.bfloat16)
    lane = lax.broadcasted_iota(jnp.int32, (1, spread_width), 1) % per_row
    picks = [jnp.where(lane == h, 1.0, 0.0).astype(jnp.bfloat16) for h in range(per_row)]

    def add(weights):
        half = chunks // 2
        sums = []
        for side in range(2):
            total = 0
            for c in range(side * half, (side + 1) * half, SPANS):
                left = []
                for u in range(c, c + SPANS):
                    piece = wide[u * rows : (u + 1) * rows]
                    left.append(jnp.concatenate([piece * pick for pick in picks], axis=0))
                left = jnp.concatenate(left, axis=1)
                right = weights[c * spread_width : (c + SPANS) * spread_width, :]
                total = total + jnp.dot(left, right, preferred_element_type=jnp.float32)
            sums.append(total)
        return sums[0] + sums[1]

    across = (((1,), (1,)), ((), ()))
    kept_kv = add(old_kv)
    values = features[:, :part_width]
    new_q = lax.dot_general(fresh_q[...], values, across, preferred_element_type=jnp.float32).T
    new_kv = lax.dot_general(fresh_kv[...], values, across, preferred_element_type=jnp.float32).T
    kept_q = add(old_q)
    stale = features[:, part_width : part_width + 1].astype(jnp.float32) == 1.0
    for j in range(per_row):
        span = slice(j * LANES, (j + 1) * LANES)
        staged[j * rows : (j + 1) * rows, :] = jnp.where(stale, kept_q[j * rows : (j + 1) * rows], new_q[:, span])
    kept = kept_kv[:rows]
    for h in range(1, per_row):
        kept = jnp.where(mine == h, kept_kv[h * rows : (h + 1) * rows], kept)
    staged[per_row * rows :, :] = jnp.where(stale, kept, new_kv)
    parts = per_row + 1
    rows_here = group_rows // n_rep
    for k in range(n_grp):
        group = jnp.bitwise_xor(mine, k)
        for r in range(n_rep):
            for i in range(rows_here):
                row = k * group_rows + r * rows_here + i
                block = staged[pl.ds(row, parts, stride=rows), :]
                for m in range(n_mp):
                    first = (m * rows_here + i) * parts
                    out[group * n_rep + r, first : first + parts, :] = block


def attend_kernel(sizes, scale, order, stale, lengths, held, keys, values, *refs):
    n_grp, n_rep, n_mp = sizes
    outs = refs[:n_mp]
    summed, turned, queries, slots, packed = refs[n_mp:]
    rows_here, places, head_size = keys.shape
    slots_here = n_grp
    heads_here = queries.shape[0] // (rows_here * n_mp)
    head_count = heads_here * n_mp
    kv_heads = slots_here * n_mp // 2
    per_group = head_count // kv_heads
    shares = heads_here // n_grp
    parts = shares + 1
    block = held.shape[1]
    step = head_size // n_grp
    mp = lax.axis_index("mp")
    rep = lax.axis_index("rep")
    sums = []
    for g in range(n_grp):
        total = held[g * n_rep]
        for r in range(1, n_rep):
            total = total + held[g * n_rep + r]
        sums.append(total)
        summed[g * block : (g + 1) * block, :] = total
    lane = lax.broadcasted_iota(jnp.int32, (1, head_size), 1) // step
    for h in range(n_grp):
        total = sums[h]
        for g in range(n_grp):
            if g != h:
                total = jnp.where(lane == g, pltpu.roll(sums[g], (step * (g - h)) % head_size, 1), total)
        turned[h * block : (h + 1) * block, :] = total
    lanes = lax.broadcasted_iota(jnp.int32, (SUBLANES, places), 1)
    head_of = lanes % kv_heads
    place_of = mp * (places // kv_heads) + lanes // kv_heads
    fields = 2 * rows_here
    stats_lane = lax.broadcasted_iota(jnp.int32, (1, LANES), 1) // (LANES // fields)
    stats = [jnp.zeros((per_group, LANES), jnp.float32) for _ in range(kv_heads)]
    for i in range(rows_here):
        flag = jnp.int32(0)
        for n in range(order.shape[0]):
            flag = jnp.where(order[n] == rep * rows_here + i, stale[n], flag)

        @pl.when(flag == 1)
        def _():
            for m in range(n_mp):
                base = (m * rows_here + i) * parts
                for g in range(n_grp):
                    first = i * head_count + m * heads_here + g * shares
                    queries[first : first + shares, :] = summed[g * block + base : g * block + base + shares, :]
                first = i * n_mp * slots_here + m * slots_here
                slots[first : first + slots_here, :] = summed[pl.ds(base + shares, slots_here, stride=block), :]

        @pl.when(flag != 1)
        def _():
            for m in range(n_mp):
                base = (m * rows_here + i) * parts
                for j in range(shares):
                    first = i * head_count + m * heads_here + j * n_grp
                    queries[first : first + n_grp, :] = turned[pl.ds(base + j, n_grp, stride=block), :]
                first = i * n_mp * slots_here + m * slots_here
                slots[first : first + slots_here, :] = turned[pl.ds(base + shares, slots_here, stride=block), :]

        query = queries[i * head_count : (i + 1) * head_count, :].astype(jnp.bfloat16)
        fresh = slots[i * 2 * kv_heads : (i + 1) * 2 * kv_heads, :].astype(jnp.bfloat16).astype(jnp.float32)
        scores = lax.dot_general(query, keys[i], (((1,), (1,)), ((), ())), preferred_element_type=jnp.float32)
        head_here = jnp.where(place_of < lengths[i], head_of, -1)
        weights, added = [], []
        for b in range(kv_heads):
            span = slice(b * per_group, (b + 1) * per_group)
            mine = jnp.sum(query[span].astype(jnp.float32) * fresh[b : b + 1], axis=1, keepdims=True)
            mine = jnp.where(mp == 0, mine, NEVER)
            held_scores = jnp.where(head_here == b, scores[span], NEVER)
            top = jnp.maximum(jnp.max(held_scores, axis=1, keepdims=True), mine)
            base = jnp.where(top == NEVER, 0.0, top)
            probable = jnp.exp2((held_scores - base) * scale)
            own = jnp.exp2((mine - base) * scale)
            total = jnp.sum(probable, axis=1, keepdims=True) + own
            weights.append(probable)
            added.append(own * fresh[kv_heads + b : kv_heads + b + 1])
            for n, value in enumerate((top, total)):
                stats[b] = jnp.where(stats_lane == 2 * i + n, value, stats[b])
        weight = jnp.concatenate(weights, axis=0).astype(jnp.bfloat16)
        out = jnp.dot(weight, values[i], preferred_element_type=jnp.float32) + jnp.concatenate(added, axis=0)
        for m in range(n_mp):
            packed[m, i * heads_here : (i + 1) * heads_here, :] = out[m * heads_here : (m + 1) * heads_here]
    for m in range(n_mp):
        here = jnp.concatenate(stats[m * heads_here // per_group : (m + 1) * heads_here // per_group], axis=0)
        packed[m, rows_here * heads_here :, :] = here
    for k, ref in enumerate(outs):
        ref[...] = packed[jnp.bitwise_xor(mp, k)]


def join_kernel(scale, *refs):
    parts, out = refs[:-1], refs[-1]
    rows_here, heads_here, head_size = out.shape
    step = LANES // (2 * rows_here)
    values = [p[...] for p in parts]
    stats = [v[rows_here * heads_here :, :] for v in values]

    def field(block, n):
        return block[:, n * step : n * step + 1]

    for i in range(rows_here):
        tops = [field(block, 2 * i) for block in stats]
        joined = functools.reduce(jnp.maximum, tops)
        scales = [jnp.exp2((top - joined) * scale) for top in tops]
        numerator = sum(v[i * heads_here : (i + 1) * heads_here, :] * s for v, s in zip(values, scales))
        divisor = sum(field(block, 2 * i + 1) * s for block, s in zip(stats, scales))
        out[i] = (numerator / divisor).astype(out.dtype)


def exchanged(value, axis, count):
    return [value] + [lax.ppermute(value, axis, [(i, i ^ k) for i in range(count)]) for k in range(1, count)]


def close(
    sizes, inputs, stale_rows, row_order, lengths, old_q, old_kv, fresh_q, fresh_kv, key_cache, value_cache
):
    n_grp, n_rep, n_mp = sizes
    group_rows, part_width = inputs.shape
    heads_here = old_q.shape[1]
    head_size = old_q.shape[2]
    slice_here = fresh_q.shape[2]
    rows = group_rows * n_grp
    rows_here, positions_here, kv_heads, _ = key_cache.shape
    shares = heads_here // n_grp
    parts = shares + 1
    bf16 = functools.partial(jax.ShapeDtypeStruct, dtype=jnp.bfloat16)
    f32 = functools.partial(jax.ShapeDtypeStruct, dtype=jnp.float32)
    moved = pl.pallas_call(
        order_kernel,
        out_shape=bf16((group_rows, part_width + LANES)),
        in_specs=[whole_block(HBM)] * 4,
        out_specs=whole_block(VMEM),
        scratch_shapes=[
            pltpu.SMEM((group_rows,), jnp.int32),
            pltpu.SMEM((group_rows,), jnp.int32),
            pltpu.VMEM((group_rows, part_width), jnp.bfloat16),
            pltpu.SemaphoreType.DMA((3,)),
        ],
        compiler_params=pltpu.CompilerParams(vmem_limit_bytes=ROOMY),
        cost_estimate=pl.CostEstimate(flops=0, bytes_accessed=START_BYTES, transcendentals=0),
        name="order",
    )(row_order, stale_rows, inputs, old_q)
    gathered = exchanged(moved, "grp", n_grp)
    near = (
        old_kv.reshape(part_width * n_grp, head_size),
        jnp.transpose(fresh_q, (1, 2, 0)).reshape(heads_here * slice_here, part_width),
        jnp.transpose(fresh_kv, (1, 2, 0)).reshape(n_grp * slice_here, part_width),
    )
    near_q = pl.pallas_call(
        load_kernel,
        out_shape=bf16((part_width, shares, head_size)),
        in_specs=[whole_block(HBM)] + [whole_block(VMEM)] * 3,
        out_specs=whole_block(pl.ANY),
        scratch_shapes=[pltpu.SemaphoreType.DMA],
        compiler_params=pltpu.CompilerParams(vmem_limit_bytes=LOAD_LIMIT),
        name="load",
    )(old_q.reshape(part_width, n_grp, shares, head_size), *near)
    block = n_mp * rows_here * parts
    terms = pl.pallas_call(
        functools.partial(project_kernel, n_rep, n_mp),
        out_shape=f32((n_grp * n_rep, block, head_size)),
        in_specs=[whole_block(VMEM)] * (n_grp + 4),
        out_specs=whole_block(VMEM),
        scratch_shapes=[
            pltpu.VMEM((rows, part_width + LANES), jnp.bfloat16),
            pltpu.VMEM((rows * parts, LANES), jnp.float32),
        ],
        compiler_params=pltpu.CompilerParams(vmem_limit_bytes=PROJECT_LIMIT),
        name="project",
    )(*gathered, near_q.reshape(part_width * shares, head_size), *near)
    devices = n_grp * n_rep * n_mp
    held = lax.all_to_all(terms.reshape(devices, 1, rows_here * parts * head_size), AXES, 0, 0, tiled=True)
    held = held.reshape(n_grp * n_rep, block, head_size)
    places = positions_here * kv_heads
    packed_rows = (rows_here + 1) * heads_here
    scale = math.log2(math.e) / math.sqrt(head_size)
    partial_out = pl.pallas_call(
        functools.partial(attend_kernel, sizes, scale),
        out_shape=[f32((packed_rows, LANES))] * n_mp,
        in_specs=[whole_block(SMEM)] * 3 + [whole_block(VMEM)] * 3,
        out_specs=[whole_block(VMEM)] * n_mp,
        scratch_shapes=[
            pltpu.VMEM((n_grp * block, LANES), jnp.float32),
            pltpu.VMEM((n_grp * block, LANES), jnp.float32),
            pltpu.VMEM((rows_here * heads_here * n_mp, LANES), jnp.float32),
            pltpu.VMEM((rows_here * 2 * kv_heads, LANES), jnp.float32),
            pltpu.VMEM((n_mp, packed_rows, LANES), jnp.float32),
        ],
        compiler_params=pltpu.CompilerParams(vmem_limit_bytes=16 << 20),
        name="attend",
    )(
        row_order,
        stale_rows,
        lengths,
        held,
        key_cache.reshape(rows_here, places, head_size),
        value_cache.reshape(rows_here, places, head_size),
    )
    pieces = [partial_out[0]] + [
        lax.ppermute(partial_out[k], "mp", [(i, i ^ k) for i in range(n_mp)]) for k in range(n_mp - 1, 0, -1)
    ]
    return pl.pallas_call(
        functools.partial(join_kernel, scale),
        out_shape=bf16((rows_here, heads_here, head_size)),
        in_specs=[whole_block(VMEM)] * n_mp,
        out_specs=whole_block(VMEM),
        compiler_params=pltpu.CompilerParams(vmem_limit_bytes=4 << 20),
        name="join",
    )(*pieces)


def fits(sizes, old_q, old_kv, fresh_q, key_cache):
    n_grp, n_rep, n_mp = sizes
    heads_here, head_size = old_q.shape[1:]
    slots_here = old_kv.shape[1]
    rows_here, _, kv_heads, _ = key_cache.shape
    return (
        head_size == LANES
        and slots_here == n_grp
        and heads_here == n_grp * n_grp
        and fresh_q.shape[2] * n_grp == head_size
        and n_grp & (n_grp - 1) == 0
        and n_mp & (n_mp - 1) == 0
        and heads_here * n_mp == SUBLANES * kv_heads
        and heads_here % SUBLANES == 0
        and slots_here * n_mp == 2 * kv_heads
        and n_mp * rows_here * (n_grp + 1) % SUBLANES == 0
        and LANES // (2 * rows_here) > 0
        and n_grp * n_rep * rows_here % (2 * SUBLANES) == 0
        and old_q.shape[0] % (2 * SPANS * LANES) == 0
    )


def local(sizes, *args):
    old_q, old_kv, fresh_q, key_cache = args[4], args[5], args[6], args[8]
    return (close if fits(sizes, old_q, old_kv, fresh_q, key_cache) else plain)(sizes, *args)


def solution(mesh):
    sizes = tuple(mesh.shape[a] for a in AXES)
    return jax.shard_map(
        functools.partial(local, sizes),
        mesh=mesh,
        in_specs=(
            P("grp", "rep"),
            P("grp"),
            P("grp"),
            P(("grp", "rep")),
            P("rep", "mp", None),
            P("rep", "mp", None),
            P("rep", "mp", "grp"),
            P("rep", "mp", "grp"),
            P(("grp", "rep"), "mp", None, None),
            P(("grp", "rep"), "mp", None, None),
        ),
        out_specs=P(("grp", "rep"), "mp", None),
        check_vma=False,
    )
```
